32 devices in a mesh: by: 4 (over y, core), bx: 8 (over z, x).
Axes of the slice: x: 2, y: 2, z: 4, core: 2. Of those that a mesh axis runs over, the one named last changes fastest.
Arguments:
- fields: float32 [3, 8, 1024, 2048], P(None, None, 'by', 'bx'), may hold values from -6 to 6
- level_count: int32 [1024, 2048], P('by', 'bx'), may hold values from 0 to 8, as said below
- thickness: float32 [8], replicated, may hold values from 0.05 to 0.3
- old_pressure: float32 [1024, 2048], P('by', 'bx'), may hold values from -6 to 6
Outputs:
- pressure: float32 [1024, 2048], P('by', 'bx')
- residual: float32 [1024, 2048], P('by', 'bx')
The draws below stay inside these ranges and needn't reach their ends.
Inputs may be any that keep to these rules, and one draw needn't show every extreme that they name: `level_count`: land comes in aligned squares of 8 x 8 cells, except that the cell at row 1, column 0 is always ocean with all 8 levels.
All inputs are finite; a program needn't handle non-finite values.
Results may differ from the reference program's by a relative error of at most 0.00024.
Values sent between devices are 32-bit elements; how exact they have to be, the bound alone decides.
No kernel may reach another device: no remote copies, remote signals or barrier semaphores. Data moves between devices by JAX's collectives and lax.ppermute only.
A program may use at most 128 MiB of HBM per device.

```python
import math
import jax
import jax.numpy as jnp
from jax import lax

KM = 8
ITERS = 4
NX = 2048
NY = 1024


def draw_level_count(key, part):
    key_land = jax.random.fold_in(key, 11)
    key_levels = jax.random.fold_in(key, 23)
    coarse = jax.random.randint(key_land, (NY // 8, NX // 8), 0, 100)
    land = jnp.repeat(jnp.repeat(coarse < 30, 8, axis=0), 8, axis=1)
    levels = jax.random.randint(key_levels, (NY, NX), 1, KM + 1)
    counts = jnp.where(land, 0, levels)
    counts = counts.at[1, 0].set(KM)
    return counts.astype(jnp.int32)


def level_of(own_key, shape, cuts, least, top_value):
    def one(dim, parts):
        steps = jax.random.uniform(jax.random.fold_in(jax.random.fold_in(own_key, 6), dim), (parts,), jnp.float32, least / len(cuts), top_value / len(cuts))
        return jnp.repeat(jnp.exp(steps), shape[dim] // parts).reshape((-1,) + (1,) * (len(shape) - dim - 1))

    gain = one(*cuts[0])
    for cut in cuts[1:]:
        gain = gain * one(*cut)
    return gain


def normal_values(key, dims, spread, reach, shards=(), kind=jnp.bfloat16):
    drawn = jax.random.normal(key, dims, jnp.float32) * spread
    if len(shards) > 0:
        drawn = level_of(key, dims, shards, -0.22, 0.18) * drawn
    return jnp.clip(drawn, min=-reach, max=reach).astype(kind)


def setup_inputs(seed: int = 0) -> dict:
    key_of = jax.random.split(jax.random.key(seed), 5)
    fields = normal_values(key_of[0], (3, KM, NY, NX), 1.0, 6.0, ((2, 4), (3, 8)), jnp.float32)
    level_count = draw_level_count(jax.random.fold_in(key_of[4], 71), 0)
    thickness = jnp.clip(jnp.exp(jax.random.uniform(key_of[2], (KM,), jnp.float32, math.log(0.05), math.log(0.3))), 0.05, 0.3)
    old_pressure = normal_values(key_of[3], (NY, NX), 1.0, 6.0, ((0, 4), (1, 8)), jnp.float32)
    return {"fields": fields, "level_count": level_count, "thickness": thickness, "old_pressure": old_pressure}


VISCOSITY = 0.05
IMPLICIT = 0.05


def laplace(field):
    return (field[..., 1:-1, 2:] + field[..., 1:-1, :-2] + field[..., 2:, 1:-1]
            + field[..., :-2, 1:-1] - 4.0 * field[..., 1:-1, 1:-1])


def level_divergence(extended):
    zonal = extended[0]
    meridional = extended[1]
    baroclinic = extended[2]
    tend_zonal = -VISCOSITY * laplace(laplace(zonal)) - 0.5 * (baroclinic[..., 2:-2, 3:-1] - baroclinic[..., 2:-2, 1:-3])
    tend_merid = -VISCOSITY * laplace(laplace(meridional)) - 0.5 * (baroclinic[..., 3:-1, 2:-2] - baroclinic[..., 1:-3, 2:-2])
    return (0.5 * (tend_zonal[..., 1:-1, 2:] - tend_zonal[..., 1:-1, :-2])
            + 0.5 * (tend_merid[..., 2:, 1:-1] - tend_merid[..., :-2, 1:-1]))


def corner_min(extended_depth):
    return jnp.minimum(jnp.minimum(extended_depth[:-1, :-1], extended_depth[:-1, 1:]),
                       jnp.minimum(extended_depth[1:, :-1], extended_depth[1:, 1:]))


def operate(extended, corner):
    west_south = extended[:-1, :-1]
    east_south = extended[:-1, 1:]
    west_north = extended[1:, :-1]
    east_north = extended[1:, 1:]
    east_slope = 0.5 * (east_south + east_north - west_south - west_north)
    north_slope = 0.5 * (west_north + east_north - west_south - east_south)
    plus_flux = 0.5 * corner * (east_slope + north_slope)
    minus_flux = 0.5 * corner * (east_slope - north_slope)
    return (IMPLICIT * extended[1:-1, 1:-1] + plus_flux[:-1, :-1] - plus_flux[1:, 1:]
            + minus_flux[1:, :-1] - minus_flux[:-1, 1:])


def wrap_pad(field):
    return jnp.pad(field, 1, mode="wrap")


def reference(fields, level_count, thickness, old_pressure):
    def level_body(level, carry):
        total, depth_sum = carry
        layer = lax.dynamic_index_in_dim(fields, level, axis=1, keepdims=False)
        padded = jnp.pad(layer, ((0, 0), (3, 3), (3, 3)), mode="wrap")
        wet_mask = (level < level_count).astype(jnp.float32)
        weight = thickness[level] * wet_mask
        return total + weight * level_divergence(padded), depth_sum + weight

    zeros_field = jnp.zeros(old_pressure.shape, jnp.float32)
    forcing_sum, column_depth = lax.fori_loop(0, KM, level_body, (zeros_field, zeros_field))
    ocean_mask = (level_count > 0).astype(jnp.float32)
    right_side = ocean_mask * (forcing_sum + IMPLICIT * old_pressure)
    pressure = ocean_mask * old_pressure
    corner = corner_min(wrap_pad(column_depth))
    diagonal = IMPLICIT + 0.5 * (corner[1:, 1:] + corner[1:, :-1] + corner[:-1, 1:] + corner[:-1, :-1])
    residual = right_side - operate(wrap_pad(pressure), corner)
    precond = residual / diagonal
    direction = precond
    norm_now = jnp.sum(residual * precond)
    for iteration in range(ITERS):
        image_field = operate(wrap_pad(direction), corner)
        step_length = norm_now / jnp.sum(direction * image_field)
        pressure = pressure + step_length * direction
        residual = residual - step_length * image_field
        precond = residual / diagonal
        norm_next = jnp.sum(residual * precond)
        direction = precond + (norm_next / norm_now) * direction
        norm_now = norm_next
    return pressure, residual
```

```python
import functools

import jax
import jax.numpy as jnp
from jax import lax
from jax.experimental import pallas as pl
from jax.experimental.pallas import tpu as pltpu
from jax.sharding import PartitionSpec as P

ITERS = 4
VISCOSITY = 0.05
IMPLICIT = 0.05

ROWS = 8
PAD = 8
LANES = 128
REACH = 3
DEEP = ITERS
EDGE = ITERS + 1

OUT_AT = 0
VMEM = pltpu.VMEM


def message_rows(levels):
    forcing_at = REACH * levels
    count_at = forcing_at + DEEP
    pressure_at = count_at + EDGE
    total = pressure_at + EDGE
    return forcing_at, count_at, pressure_at, -(-total // 8) * 8


def east(value):
    return pltpu.roll(value, value.shape[1] - 1, 1)


def west(value):
    return pltpu.roll(value, 1, 1)


def lane_index(rows):
    return lax.broadcasted_iota(jnp.int32, (rows, LANES), 1)


def forcing_kernel(
    thick, fields, south, north, count, old, part, depth, guess, to_east, to_west,
    zonal, merid, baro, mixed, lap, wet, pack_e, pack_w,
):
    level = pl.program_id(0)
    levels = pl.num_programs(0)
    static_levels = (south.shape[0] - 2) // 3
    height, width = count.shape
    ext = height + 2 * ROWS
    full = width + LANES
    base = PAD + ROWS
    forcing_at, count_at, pressure_at, _ = message_rows(static_levels)

    @pl.when(level == 0)
    def _():
        for buf in (zonal, merid, baro):
            buf[:, width:] = jnp.zeros((ext + 2 * PAD, LANES), jnp.float32)
        for buf in (zonal, merid, baro, mixed, lap):
            buf[:PAD, :] = jnp.zeros((PAD, full), jnp.float32)
            buf[PAD + ext :, :] = jnp.zeros((PAD, full), jnp.float32)
        part[...] = jnp.zeros_like(part)
        depth[...] = jnp.zeros_like(depth)
        pack_e[...] = jnp.zeros_like(pack_e)
        pack_w[...] = jnp.zeros_like(pack_w)
        wet[:ROWS, :] = south[3 * static_levels]
        wet[ROWS : ROWS + height, :] = count[...].astype(jnp.float32)
        wet[ROWS + height :, :] = north[3 * static_levels]

    for which, buf in enumerate((zonal, merid, baro)):
        buf[PAD:base, :width] = south[which * static_levels + level]
        buf[base : base + height, :width] = fields[which, 0]
        buf[base + height : base + height + ROWS, :width] = north[which * static_levels + level]

    step = 8
    starts = range(PAD, PAD + ext, step)
    for r in starts:
        row = zonal[r : r + step, :]
        up = merid[r + 1 : r + 1 + step, :]
        down = merid[r - 1 : r - 1 + step, :]
        mixed[r : r + step, :] = (east(row) - west(row)) + (up - down)
    for r in starts:
        row = mixed[r : r + step, :]
        lap[r : r + step, :] = (
            (east(row) + west(row))
            + (mixed[r + 1 : r + 1 + step, :] + mixed[r - 1 : r - 1 + step, :])
            - 4.0 * row
        )
    thickness = thick[level]
    level_number = level.astype(jnp.float32)
    lane = lane_index(step)
    for r in starts:
        row = lap[r : r + step, :]
        second = (
            (east(row) + west(row))
            + (lap[r + 1 : r + 1 + step, :] + lap[r - 1 : r - 1 + step, :])
            - 4.0 * row
        )
        centre = baro[r : r + step, :]
        spread = (
            (pltpu.roll(centre, full - 2, 1) + pltpu.roll(centre, 2, 1))
            + (baro[r + 2 : r + 2 + step, :] + baro[r - 2 : r - 2 + step, :])
            - 4.0 * centre
        )
        div = (-0.5 * VISCOSITY) * second - 0.25 * spread
        e = r - PAD
        weight = jnp.where(wet[e : e + step, :] > level_number, thickness, 0.0)
        part[e : e + step, :] += weight * div[:, :width]
        depth[e : e + step, :] += weight
        outside = div[:, width:]
        going_east = jnp.where(lane < REACH, outside, 0.0)
        going_west = jnp.where(lane >= LANES - REACH, outside, 0.0)
        pack_e[e : e + step, :] += pltpu.roll(going_east, REACH * level, 1)
        pack_w[e : e + step, :] += pltpu.roll(going_west, REACH * level + REACH, 1)

    @pl.when(level == levels - 1)
    def _():
        for e in range(0, ext, step):
            if e < ROWS:
                pressure = south[3 * static_levels + 1]
            elif e >= ROWS + height:
                pressure = north[3 * static_levels + 1]
            else:
                pressure = old[e - ROWS : e - ROWS + step, :]
            start = jnp.where(depth[e : e + step, :] > 0.0, pressure, 0.0)
            guess[e : e + step, :] = start
            for pack, at, inner in ((pack_e, width - LANES, True), (pack_w, 0, False)):
                tile = pack[e : e + step, :]
                pieces = (
                    (part[e : e + step, at : at + LANES], forcing_at, DEEP),
                    (wet[e : e + step, at : at + LANES], count_at, EDGE),
                    (start[:, at : at + LANES], pressure_at, EDGE),
                )
                for piece, lane_at, size in pieces:
                    shift = lane_at + size if inner else lane_at
                    moved = pltpu.roll(piece, shift, 1)
                    inside = (lane >= lane_at) & (lane < lane_at + size)
                    tile = jnp.where(inside, moved, tile)
                pack[e : e + step, :] = tile
        for pack, message in ((pack_e, to_east), (pack_w, to_west)):
            for at in range(0, message.shape[1], LANES):
                turned = jnp.transpose(pack[at : at + LANES, :])
                message[:, at : at + LANES] = turned[: message.shape[0], :]


def solve_kernel(
    thick, part, depth, guess, to_east, to_west, from_west, from_east,
    base0, base1, base2, base3, base4, diag_out, moments,
    turned, deep, start, half, half_w, diag, inverse, right, vec_a, vec_b,
):
    ext, width = part.shape
    height = ext - 2 * ROWS
    full = width + LANES
    levels = thick.shape[0]
    forcing_at, count_at, pressure_at, _ = message_rows(levels)

    def weights(counts):
        return [jnp.where(counts > float(k), thick[k], 0.0) for k in range(levels)]

    def weighted(counts, message):
        total = None
        for k, weight in enumerate(weights(counts)):
            term = weight * message[REACH * k : REACH * k + REACH, :]
            total = term if total is None else total + term
        return total

    def rows(message, at, size):
        return message[at : at + size, :]

    skip = EDGE - REACH
    turned[...] = jnp.zeros_like(turned)
    edge_forcing = rows(from_east, forcing_at, DEEP)
    turned[0:DEEP, :] = edge_forcing
    turned[0:REACH, :] += weighted(rows(from_east, count_at, REACH), to_east)
    turned[LANES - DEEP : LANES, :] = rows(from_west, forcing_at, DEEP)
    turned[LANES - REACH : LANES, :] += weighted(rows(from_west, count_at + skip, REACH), to_west)
    turned[40 : 40 + EDGE, :] = sum(weights(rows(from_east, count_at, EDGE)))
    turned[40 - EDGE : 40, :] = sum(weights(rows(from_west, count_at, EDGE)))
    turned[60 : 60 + EDGE, :] = rows(from_east, pressure_at, EDGE)
    turned[60 - EDGE : 60, :] = rows(from_west, pressure_at, EDGE)
    turned[80 : 80 + REACH, :] = weighted(rows(to_west, count_at, REACH), from_west)
    turned[80 - REACH : 80, :] = weighted(rows(to_east, count_at + skip, REACH), from_east)

    step = 8
    lane = lane_index(step)
    for buf in (deep, start, half, half_w, vec_a, vec_b):
        buf[:PAD, :] = jnp.zeros((PAD, full), jnp.float32)
        buf[PAD + ext :, :] = jnp.zeros((PAD, full), jnp.float32)
    for at in range(0, ext, LANES):
        block = jnp.transpose(turned[:, at : at + LANES])
        for e in range(at, min(at + LANES, ext), step):
            r = e + PAD
            tile = block[e - at : e - at + step, :]
            near = (lane < EDGE) | (lane >= LANES - EDGE)
            deep[r : r + step, :width] = depth[e : e + step, :]
            deep[r : r + step, width:] = jnp.where(near, pltpu.roll(tile, LANES - 40, 1), 0.0)
            start[r : r + step, :width] = guess[e : e + step, :]
            start[r : r + step, width:] = jnp.where(near, pltpu.roll(tile, LANES - 60, 1), 0.0)
            fix = pltpu.roll(tile, LANES - 80, 1)
            right[e : e + step, :width] = part[e : e + step, :]
            right[e : e + step, :LANES] += jnp.where(lane < REACH, fix, 0.0)
            right[e : e + step, width - LANES : width] += jnp.where(lane >= LANES - REACH, fix, 0.0)
            close = (lane < DEEP) | (lane >= LANES - DEEP)
            right[e : e + step, width:] = jnp.where(close, tile, 0.0)

    starts = range(PAD, PAD + ext, step)
    for r in starts:
        here = deep[r : r + step, :]
        above = deep[r + 1 : r + 1 + step, :]
        low = jnp.minimum(here, above)
        corner = 0.5 * jnp.minimum(low, east(low))
        half[r : r + step, :] = corner
        half_w[r : r + step, :] = west(corner)

    for r in starts:
        e = r - PAD
        ch = half[r : r + step, :]
        chw = half_w[r : r + step, :]
        ch_s = half[r - 1 : r - 1 + step, :]
        chw_s = half_w[r - 1 : r - 1 + step, :]
        diagonal = IMPLICIT + ((ch + chw) + (ch_s + chw_s))
        inv = 1.0 / diagonal
        diag[e : e + step, :] = diagonal
        inverse[e : e + step, :] = inv
        here = start[r : r + step, :]
        up = start[r + 1 : r + 1 + step, :]
        down = start[r - 1 : r - 1 + step, :]
        image = IMPLICIT * here + (
            (ch * (here - east(up)) + chw * (here - west(up)))
            + (ch_s * (here - east(down)) + chw_s * (here - west(down)))
        )
        side = jnp.where(
            deep[r : r + step, :] > 0.0, right[e : e + step, :] + IMPLICIT * here, 0.0
        )
        vec_a[r : r + step, :] = (side - image) * inv

    outs = (base0, base1, base2, base3, base4)
    for r in starts:
        e = r - PAD
        if ROWS <= e < ROWS + height:
            o = e - ROWS
            base0[o : o + step, :] = vec_a[r : r + step, :width]
            diag_out[o : o + step, :] = diag[e : e + step, :width]
    buffers = (vec_a, vec_b)
    sums = []
    for j in range(ITERS):
        source, target = buffers[j % 2], buffers[(j + 1) % 2]
        even = jnp.zeros((step, LANES), jnp.float32)
        odd = jnp.zeros((step, LANES), jnp.float32)
        for r in starts:
            e = r - PAD
            up = source[r + 1 : r + 1 + step, :]
            down = source[r - 1 : r - 1 + step, :]
            value = inverse[e : e + step, :] * (
                (half[r : r + step, :] * east(up) + half_w[r : r + step, :] * west(up))
                + (
                    half[r - 1 : r - 1 + step, :] * east(down)
                    + half_w[r - 1 : r - 1 + step, :] * west(down)
                )
            )
            target[r : r + step, :] = value
            if ROWS <= e < ROWS + height:
                o = e - ROWS
                inner = value[:, :width]
                outs[j + 1][o : o + step, :] = inner
                now = source[r : r + step, :width]
                scaled = diag[e : e + step, :width] * now
                first = scaled * now
                second = scaled * inner
                for at in range(0, width, LANES):
                    even = even + first[:, at : at + LANES]
                    odd = odd + second[:, at : at + LANES]
        sums += [even, odd]
    lane_row = lax.broadcasted_iota(jnp.int32, (1, LANES), 1)
    found = jnp.zeros((1, LANES), jnp.float32)
    for m, acc in enumerate(sums):
        found = jnp.where(lane_row == m, jnp.sum(acc), found)
    for d in range(moments.shape[0]):
        moments[d] = found


def combine_kernel(moments, guess, base0, base1, base2, base3, base4, diag, pressure, residual):
    height, width = pressure.shape
    step = 8
    total = jnp.sum(moments[...], axis=0)
    shape = (step, width)
    h = [jnp.broadcast_to(total[:, m : m + 1], (step, LANES)) for m in range(2 * ITERS)]
    one, zero = jnp.ones((step, LANES), jnp.float32), None

    def plus(a, b):
        return b if a is None else a if b is None else a + b

    def times(a, b):
        return None if a is None or b is None else a * b

    def minus_n(poly):
        moved = [zero] + list(poly)
        return [
            a if b is None else (-b if a is None else a - b)
            for a, b in zip(list(poly) + [zero], moved)
        ]

    def inner(left, right):
        total = None
        for i, a in enumerate(left):
            part = None
            for j, b in enumerate(right):
                part = plus(part, times(b, h[i + j]))
            total = plus(total, times(a, part))
        return total

    rest, direction, answer = [one], [one], []
    norm = h[0]
    for iteration in range(ITERS):
        image = minus_n(direction)
        alpha = norm / inner(direction, image)
        answer = [
            plus(answer[i] if i < len(answer) else None, alpha * c)
            for i, c in enumerate(direction)
        ]
        rest = [
            plus(rest[i] if i < len(rest) else None, -(alpha * c)) for i, c in enumerate(image)
        ]
        if iteration + 1 < ITERS:
            following = inner(rest, rest)
            ratio = following / norm
            direction = [
                plus(c, ratio * direction[i] if i < len(direction) else None)
                for i, c in enumerate(rest)
            ]
            norm = following
    spread = lambda c: jnp.broadcast_to(c[:1, :1], shape)
    answer = [spread(c) for c in answer]
    rest = [spread(c) for c in rest]
    bases = (base0, base1, base2, base3, base4)
    for o in range(0, height, step):
        vecs = [b[o : o + step, :] for b in bases]
        moved = sum(c * v for c, v in zip(answer, vecs))
        left = sum(c * v for c, v in zip(rest, vecs))
        pressure[o : o + step, :] = guess[ROWS + o : ROWS + o + step, :] + moved
        residual[o : o + step, :] = diag[o : o + step, :] * left


def shift(value, axis, by):
    size = lax.axis_size(axis)
    return lax.ppermute(value, axis, [(i, (i + by) % size) for i in range(size)])


def shards(fields, level_count, thickness, old_pressure):
    levels, height, width = fields.shape[1:]
    ext, full, tall = height + 2 * ROWS, width + LANES, height + LANES
    f32 = jnp.float32
    counts = level_count.astype(f32)

    def edge(at):
        pick = lambda a: lax.slice_in_dim(a, at, at + ROWS, axis=a.ndim - 2)
        flat = pick(fields).reshape(3 * levels, ROWS, width)
        return jnp.concatenate([flat, pick(counts)[None], pick(old_pressure)[None]], axis=0)

    south = shift(edge(height - ROWS), "by", 1)
    north = shift(edge(0), "by", -1)

    message = message_rows(levels)[3]
    smem = pl.BlockSpec(memory_space=pltpu.SMEM)
    whole = lambda *dims: pl.BlockSpec(dims, lambda k: (0,) * len(dims))
    halo = whole(3 * levels + 2, ROWS, width)
    block = whole(ext, width)
    scratch = lambda r, c: pltpu.VMEM((r, c), f32)
    part, depth, guess, to_east, to_west = pl.pallas_call(
        forcing_kernel,
        grid=(levels,),
        in_specs=[
            smem,
            pl.BlockSpec((3, 1, height, width), lambda k: (0, k, 0, 0)),
            halo, halo, whole(height, width), whole(height, width),
        ],
        out_specs=[block, block, block, whole(message, tall), whole(message, tall)],
        out_shape=[jax.ShapeDtypeStruct((ext, width), f32)] * 3
        + [jax.ShapeDtypeStruct((message, tall), f32)] * 2,
        scratch_shapes=[scratch(ext + 2 * PAD, full)] * 5
        + [scratch(ext, width)]
        + [scratch(tall, LANES)] * 2,
        name="forcing",
    )(thickness, fields, south, north, level_count, old_pressure)

    from_west = shift(to_east, "bx", 1)
    from_east = shift(to_west, "bx", -1)

    devices = lax.axis_size("by") * lax.axis_size("bx")
    vmem = pl.BlockSpec(memory_space=pltpu.VMEM)
    out = jax.ShapeDtypeStruct((height, width), f32)
    *bases, diag, moments = pl.pallas_call(
        solve_kernel,
        in_specs=[smem] + [vmem] * 7,
        out_specs=[vmem] * (ITERS + 3),
        out_shape=[out] * (ITERS + 2) + [jax.ShapeDtypeStruct((devices, 1, LANES), f32)],
        scratch_shapes=[scratch(LANES, tall)]
        + [scratch(ext + 2 * PAD, full)] * 4
        + [scratch(ext, full)] * 3
        + [scratch(ext + 2 * PAD, full)] * 2,
        name="krylov",
    )(thickness, part, depth, guess, to_east, to_west, from_west, from_east)

    moments = lax.all_to_all(moments, ("by", "bx"), split_axis=0, concat_axis=0, tiled=True)
    return tuple(
        pl.pallas_call(
            combine_kernel,
            in_specs=[vmem] * (ITERS + 4),
            out_specs=[vmem] * 2,
            out_shape=[out] * 2,
            name="combine",
        )(moments, guess, *bases, diag)
    )


def solution(mesh):
    placed = (P(None, None, "by", "bx"), P("by", "bx"), P(), P("by", "bx"))
    return jax.shard_map(
        shards,
        mesh=mesh,
        in_specs=placed,
        out_specs=(P("by", "bx"), P("by", "bx")),
        check_vma=False,
    )
```

```python
import jax
import jax.numpy as jnp
from jax import lax
from jax.experimental import pallas as pl
from jax.experimental.pallas import tpu as pltpu
from jax.sharding import PartitionSpec as P

ITERS = 4
VISCOSITY = 0.05
IMPLICIT = 0.05

ROWS = 8
PAD = 8
LANES = 128
REACH = 3
DEEP = ITERS
EDGE = ITERS + 1

STEP = 8


def message_rows(levels):
    forcing_at = REACH * levels
    count_at = forcing_at + DEEP
    pressure_at = count_at + EDGE
    total = pressure_at + EDGE
    return forcing_at, count_at, pressure_at, -(-total // 8) * 8


def lane_index():
    return lax.broadcasted_iota(jnp.int32, (STEP, LANES), 1)


def turn(value, by):
    return pltpu.roll(value, by % LANES, 1)


def neighbours(tiles, lane, by=1):
    count = len(tiles)
    back = [None if t is None else turn(t, -by) for t in tiles]
    forth = [None if t is None else turn(t, by) for t in tiles]

    def pick(mask, other, own):
        if other is None and own is None:
            return None
        zero = jnp.zeros((STEP, LANES), jnp.float32)
        return jnp.where(mask, zero if other is None else other, zero if own is None else own)

    east = [pick(lane >= LANES - by, back[(i + 1) % count], back[i]) for i in range(count)]
    west = [pick(lane < by, forth[i - 1], forth[i]) for i in range(count)]
    return east, west


def forcing_kernel(
    thick, fields, south, north, count, old, part, depth, guess, to_east, to_west,
    zonal, merid, baro, mixed, lap, wet, pack_e, pack_w,
):
    level = pl.program_id(0)
    levels = pl.num_programs(0)
    static_levels = (south.shape[0] - 2) // 3
    height, width = count.shape
    tiles = width // LANES
    ext = height + 2 * ROWS
    base = PAD + ROWS
    forcing_at, count_at, pressure_at, _ = message_rows(static_levels)
    lane = lane_index()
    cols = [pl.ds(t * LANES, LANES) for t in range(tiles)]

    def extended(e, lower, middle, upper):
        if e < ROWS:
            return lower
        if e >= ROWS + height:
            return upper
        return middle(e - ROWS)

    @pl.when(level == 0)
    def _():
        for buf in (merid, baro, mixed, lap, depth, guess):
            for at in (0, PAD + ext):
                buf[:, at : at + PAD, :] = jnp.zeros((buf.shape[0], PAD, LANES), jnp.float32)
        part[...] = jnp.zeros_like(part)
        depth[...] = jnp.zeros_like(depth)
        pack_e[...] = jnp.zeros_like(pack_e)
        pack_w[...] = jnp.zeros_like(pack_w)
        for t, c in enumerate(cols):
            wet[t, :ROWS, :] = south[3 * static_levels, :, c]
            wet[t, ROWS : ROWS + height, :] = count[:, c].astype(jnp.float32)
            wet[t, ROWS + height :, :] = north[3 * static_levels, :, c]

    for which, buf in enumerate((zonal, merid, baro)):
        for t, c in enumerate(cols):
            buf[t, PAD:base, :] = south[which * static_levels + level, :, c]
            buf[t, base : base + height, :] = fields[which, 0, :, c]
            buf[t, base + height : base + height + ROWS, :] = north[
                which * static_levels + level, :, c
            ]

    starts = range(PAD, PAD + ext, STEP)
    for r in starts:
        east, west = neighbours([zonal[t, r : r + STEP, :] for t in range(tiles)] + [None], lane)
        for t in range(tiles + 1):
            value = east[t] - west[t]
            if t < tiles:
                value += merid[t, r + 1 : r + 1 + STEP, :] - merid[t, r - 1 : r - 1 + STEP, :]
            mixed[t, r : r + STEP, :] = value

    def laplace(buf, r):
        own = [buf[t, r : r + STEP, :] for t in range(tiles + 1)]
        east, west = neighbours(own, lane)
        return [
            (east[t] + west[t])
            + (buf[t, r + 1 : r + 1 + STEP, :] + buf[t, r - 1 : r - 1 + STEP, :])
            - 4.0 * own[t]
            for t in range(tiles + 1)
        ]

    for r in starts:
        for t, value in enumerate(laplace(mixed, r)):
            lap[t, r : r + STEP, :] = value
    thickness = thick[level]
    level_number = level.astype(jnp.float32)
    for r in starts:
        e = r - PAD
        second = laplace(lap, r)
        own = [baro[t, r : r + STEP, :] for t in range(tiles)]
        east, west = neighbours(own + [None], lane, 2)
        for t in range(tiles + 1):
            spread = east[t] + west[t]
            if t < tiles:
                spread += baro[t, r + 2 : r + 2 + STEP, :] + baro[t, r - 2 : r - 2 + STEP, :]
                spread -= 4.0 * own[t]
            div = (-0.5 * VISCOSITY) * second[t] - 0.25 * spread
            if t < tiles:
                weight = jnp.where(wet[t, e : e + STEP, :] > level_number, thickness, 0.0)
                part[t, e : e + STEP, :] += weight * div
                depth[t, r : r + STEP, :] += weight
            else:
                going_east = jnp.where(lane < REACH, div, 0.0)
                going_west = jnp.where(lane >= LANES - REACH, div, 0.0)
                pack_e[e : e + STEP, :] += pltpu.roll(going_east, REACH * level, 1)
                pack_w[e : e + STEP, :] += pltpu.roll(going_west, REACH * level + REACH, 1)

    @pl.when(level == levels - 1)
    def _():
        for r in starts:
            e = r - PAD
            begin = []
            for t, c in enumerate(cols):
                pressure = extended(
                    e,
                    south[3 * static_levels + 1, :, c],
                    lambda o: old[o : o + STEP, c],
                    north[3 * static_levels + 1, :, c],
                )
                begin.append(jnp.where(depth[t, r : r + STEP, :] > 0.0, pressure, 0.0))
                guess[t, r : r + STEP, :] = begin[t]
            for pack, t, inner in ((pack_e, tiles - 1, True), (pack_w, 0, False)):
                tile = pack[e : e + STEP, :]
                pieces = (
                    (part[t, e : e + STEP, :], forcing_at, DEEP),
                    (wet[t, e : e + STEP, :], count_at, EDGE),
                    (begin[t], pressure_at, EDGE),
                )
                for piece, lane_at, size in pieces:
                    moved = turn(piece, lane_at + size if inner else lane_at)
                    inside = (lane >= lane_at) & (lane < lane_at + size)
                    tile = jnp.where(inside, moved, tile)
                pack[e : e + STEP, :] = tile
        for pack, message in ((pack_e, to_east), (pack_w, to_west)):
            for at in range(0, message.shape[1], LANES):
                turned = jnp.transpose(pack[at : at + LANES, :])
                message[:, at : at + LANES] = turned[: message.shape[0], :]


def solve_kernel(
    thick, part, depth, guess, to_east, to_west, from_west, from_east,
    base0, base1, base2, base3, base4, diag_out, moments,
    turned, fix, halo_part, halo_depth, halo_guess, half, half_w, diag, inverse,
    vec_a, vec_b, vec_e, vec_w,
):
    tiles, ext, _ = part.shape
    height = ext - 2 * ROWS
    levels = thick.shape[0]
    forcing_at, count_at, pressure_at, _ = message_rows(levels)
    lane = lane_index()

    def weights(counts):
        return [jnp.where(counts > float(k), thick[k], 0.0) for k in range(levels)]

    def weighted(counts, message):
        total = None
        for k, weight in enumerate(weights(counts)):
            term = weight * message[REACH * k : REACH * k + REACH, :]
            total = term if total is None else total + term
        return total

    def rows(message, at, size):
        return message[at : at + size, :]

    skip = EDGE - REACH
    turned[...] = jnp.zeros_like(turned)
    turned[0:DEEP, :] = rows(from_east, forcing_at, DEEP)
    turned[0:REACH, :] += weighted(rows(from_east, count_at, REACH), to_east)
    turned[LANES - DEEP : LANES, :] = rows(from_west, forcing_at, DEEP)
    turned[LANES - REACH : LANES, :] += weighted(rows(from_west, count_at + skip, REACH), to_west)
    turned[40 : 40 + EDGE, :] = sum(weights(rows(from_east, count_at, EDGE)))
    turned[40 - EDGE : 40, :] = sum(weights(rows(from_west, count_at, EDGE)))
    turned[60 : 60 + EDGE, :] = rows(from_east, pressure_at, EDGE)
    turned[60 - EDGE : 60, :] = rows(from_west, pressure_at, EDGE)
    turned[80 : 80 + REACH, :] = weighted(rows(to_west, count_at, REACH), from_west)
    turned[80 - REACH : 80, :] = weighted(rows(to_east, count_at + skip, REACH), from_east)

    for buf in (halo_depth, halo_guess):
        for at in (0, PAD + ext):
            buf[at : at + PAD, :] = jnp.zeros((PAD, LANES), jnp.float32)
    for buf in (half, half_w, vec_e, vec_w):
        for at in (0, PAD + ext):
            buf[:, at : at + PAD, :] = jnp.zeros((tiles + 1, PAD, LANES), jnp.float32)
    near = (lane < EDGE) | (lane >= LANES - EDGE)
    close = (lane < DEEP) | (lane >= LANES - DEEP)
    for at in range(0, ext, LANES):
        block = jnp.transpose(turned[:, at : at + LANES])
        for e in range(at, min(at + LANES, ext), STEP):
            r = e + PAD
            tile = block[e - at : e - at + STEP, :]
            halo_depth[r : r + STEP, :] = jnp.where(near, turn(tile, -40), 0.0)
            halo_guess[r : r + STEP, :] = jnp.where(near, turn(tile, -60), 0.0)
            halo_part[e : e + STEP, :] = jnp.where(close, tile, 0.0)
            fix[e : e + STEP, :] = turn(tile, -80)

    def read(main, halo, r):
        return [main[t, r : r + STEP, :] for t in range(tiles)] + [halo[r : r + STEP, :]]

    starts = range(PAD, PAD + ext, STEP)
    both = range(tiles + 1)
    for r in starts:
        low = [
            jnp.minimum(a, b)
            for a, b in zip(read(depth, halo_depth, r), read(depth, halo_depth, r + 1))
        ]
        east, _ = neighbours(low, lane)
        corner = [0.5 * jnp.minimum(a, b) for a, b in zip(low, east)]
        _, west = neighbours(corner, lane)
        begin = read(guess, halo_guess, r)
        begin_e, begin_w = neighbours(begin, lane)
        for t in both:
            half[t, r : r + STEP, :] = corner[t]
            half_w[t, r : r + STEP, :] = west[t]
            vec_e[t, r : r + STEP, :] = begin_e[t]
            vec_w[t, r : r + STEP, :] = begin_w[t]

    def around(t, r):
        pairs = []
        for at in (r, r - 1):
            there = at + 1 if at == r else at
            pairs.append((half[t, at : at + STEP, :], vec_e[t, there : there + STEP, :]))
            pairs.append((half_w[t, at : at + STEP, :], vec_w[t, there : there + STEP, :]))
        return pairs

    for r in starts:
        e = r - PAD
        begin = read(guess, halo_guess, r)
        wide = read(depth, halo_depth, r)
        fixes = fix[e : e + STEP, :]
        for t in both:
            pairs = around(t, r)
            (ch, ne), (chw, nw), (ch_s, se), (chw_s, sw) = pairs
            diagonal = IMPLICIT + ((ch + chw) + (ch_s + chw_s))
            inv = 1.0 / diagonal
            diag[t, e : e + STEP, :] = diagonal
            inverse[t, e : e + STEP, :] = inv
            here = begin[t]
            image = IMPLICIT * here + (
                (ch * (here - ne) + chw * (here - nw)) + (ch_s * (here - se) + chw_s * (here - sw))
            )
            total = halo_part[e : e + STEP, :] if t == tiles else part[t, e : e + STEP, :]
            if t == 0:
                total += jnp.where(lane < REACH, fixes, 0.0)
            if t == tiles - 1:
                total += jnp.where(lane >= LANES - REACH, fixes, 0.0)
            side = jnp.where(wide[t] > 0.0, total + IMPLICIT * here, 0.0)
            first = (side - image) * inv
            vec_a[t, e : e + STEP, :] = first
            if t < tiles and ROWS <= e < ROWS + height:
                o = e - ROWS
                base0[t, o : o + STEP, :] = first
                diag_out[t, o : o + STEP, :] = diagonal

    outs = (base0, base1, base2, base3, base4)
    buffers = (vec_a, vec_b)
    sums = []
    for j in range(ITERS):
        source, target = buffers[j % 2], buffers[(j + 1) % 2]
        for r in starts:
            e = r - PAD
            east, west = neighbours([source[t, e : e + STEP, :] for t in both], lane)
            for t in both:
                vec_e[t, r : r + STEP, :] = east[t]
                vec_w[t, r : r + STEP, :] = west[t]
        even = jnp.zeros((STEP, LANES), jnp.float32)
        odd = jnp.zeros((STEP, LANES), jnp.float32)
        for r in starts:
            e = r - PAD
            for t in both:
                (ch, ne), (chw, nw), (ch_s, se), (chw_s, sw) = around(t, r)
                value = inverse[t, e : e + STEP, :] * (
                    (ch * ne + chw * nw) + (ch_s * se + chw_s * sw)
                )
                if j + 1 < ITERS:
                    target[t, e : e + STEP, :] = value
                if t < tiles and ROWS <= e < ROWS + height:
                    o = e - ROWS
                    outs[j + 1][t, o : o + STEP, :] = value
                    now = source[t, e : e + STEP, :]
                    scaled = diag[t, e : e + STEP, :] * now
                    even = even + scaled * now
                    odd = odd + scaled * value
        sums += [even, odd]
    lane_row = lax.broadcasted_iota(jnp.int32, (1, LANES), 1)
    found = jnp.zeros((1, LANES), jnp.float32)
    for m, acc in enumerate(sums):
        found = jnp.where(lane_row == m, jnp.sum(acc), found)
    for d in range(moments.shape[0]):
        moments[d] = found


def combine_kernel(moments, guess, base0, base1, base2, base3, base4, diag, pressure, residual):
    height, width = pressure.shape
    total = jnp.sum(moments[...], axis=0)
    h = [jnp.broadcast_to(total[:, m : m + 1], (STEP, LANES)) for m in range(2 * ITERS)]
    one, zero = jnp.ones((STEP, LANES), jnp.float32), None

    def plus(a, b):
        return b if a is None else a if b is None else a + b

    def times(a, b):
        return None if a is None or b is None else a * b

    def minus_n(poly):
        moved = [zero] + list(poly)
        return [
            a if b is None else (-b if a is None else a - b)
            for a, b in zip(list(poly) + [zero], moved)
        ]

    def inner(left, right):
        total = None
        for i, a in enumerate(left):
            part = None
            for j, b in enumerate(right):
                part = plus(part, times(b, h[i + j]))
            total = plus(total, times(a, part))
        return total

    rest, direction, answer = [one], [one], []
    norm = h[0]
    for iteration in range(ITERS):
        image = minus_n(direction)
        alpha = norm / inner(direction, image)
        answer = [
            plus(answer[i] if i < len(answer) else None, alpha * c)
            for i, c in enumerate(direction)
        ]
        rest = [
            plus(rest[i] if i < len(rest) else None, -(alpha * c)) for i, c in enumerate(image)
        ]
        if iteration + 1 < ITERS:
            following = inner(rest, rest)
            ratio = following / norm
            direction = [
                plus(c, ratio * direction[i] if i < len(direction) else None)
                for i, c in enumerate(rest)
            ]
            norm = following
    bases = (base0, base1, base2, base3, base4)
    for t in range(width // LANES):
        for o in range(0, height, STEP):
            vecs = [b[t, o : o + STEP, :] for b in bases]
            moved = sum(c * v for c, v in zip(answer, vecs))
            left = sum(c * v for c, v in zip(rest, vecs))
            at = PAD + ROWS + o
            cols = pl.ds(t * LANES, LANES)
            pressure[o : o + STEP, cols] = guess[t, at : at + STEP, :] + moved
            residual[o : o + STEP, cols] = diag[t, o : o + STEP, :] * left


def shift(value, axis, by):
    size = lax.axis_size(axis)
    return lax.ppermute(value, axis, [(i, (i + by) % size) for i in range(size)])


def shards(fields, level_count, thickness, old_pressure):
    levels, height, width = fields.shape[1:]
    ext, tall = height + 2 * ROWS, height + LANES
    f32 = jnp.float32
    counts = level_count.astype(f32)

    def edge(at):
        pick = lambda a: lax.slice_in_dim(a, at, at + ROWS, axis=a.ndim - 2)
        flat = pick(fields).reshape(3 * levels, ROWS, width)
        return jnp.concatenate([flat, pick(counts)[None], pick(old_pressure)[None]], axis=0)

    south = shift(edge(height - ROWS), "by", 1)
    north = shift(edge(0), "by", -1)

    message = message_rows(levels)[3]
    tiles, padded = width // LANES, ext + 2 * PAD
    smem = pl.BlockSpec(memory_space=pltpu.SMEM)
    vmem = pl.BlockSpec(memory_space=pltpu.VMEM)
    whole = lambda *dims: pl.BlockSpec(dims, lambda k: (0,) * len(dims))
    halo = whole(3 * levels + 2, ROWS, width)
    shaped = lambda *dims: jax.ShapeDtypeStruct(dims, f32)
    scratch = lambda *dims: pltpu.VMEM(dims, f32)
    main = (tiles, ext, LANES)
    loose = (tiles, padded, LANES)
    results = (main, loose, loose, (message, tall), (message, tall))
    part, depth, guess, to_east, to_west = pl.pallas_call(
        forcing_kernel,
        grid=(levels,),
        in_specs=[
            smem,
            pl.BlockSpec((3, 1, height, width), lambda k: (0, k, 0, 0)),
            halo, halo, whole(height, width), whole(height, width),
        ],
        out_specs=[whole(*dims) for dims in results],
        out_shape=[shaped(*dims) for dims in results],
        scratch_shapes=[scratch(*loose)] * 3
        + [scratch(tiles + 1, padded, LANES)] * 2
        + [scratch(*main)]
        + [scratch(tall, LANES)] * 2,
        name="forcing",
    )(thickness, fields, south, north, level_count, old_pressure)

    from_west = shift(to_east, "bx", 1)
    from_east = shift(to_west, "bx", -1)

    devices = lax.axis_size("by") * lax.axis_size("bx")
    out = shaped(tiles, height, LANES)
    *bases, diag, moments = pl.pallas_call(
        solve_kernel,
        in_specs=[smem] + [vmem] * 7,
        out_specs=[vmem] * (ITERS + 3),
        out_shape=[out] * (ITERS + 2) + [shaped(devices, 1, LANES)],
        scratch_shapes=[scratch(LANES, tall), scratch(ext, LANES), scratch(ext, LANES)]
        + [scratch(padded, LANES)] * 2
        + [scratch(tiles + 1, padded, LANES)] * 2
        + [scratch(tiles + 1, ext, LANES)] * 4
        + [scratch(tiles + 1, padded, LANES)] * 2,
        name="krylov",
    )(thickness, part, depth, guess, to_east, to_west, from_west, from_east)

    moments = lax.all_to_all(moments, ("by", "bx"), split_axis=0, concat_axis=0, tiled=True)
    return tuple(
        pl.pallas_call(
            combine_kernel,
            in_specs=[vmem] * (ITERS + 4),
            out_specs=[vmem] * 2,
            out_shape=[shaped(height, width)] * 2,
            name="combine",
        )(moments, guess, *bases, diag)
    )


def solution(mesh):
    placed = (P(None, None, "by", "bx"), P("by", "bx"), P(), P("by", "bx"))
    return jax.shard_map(
        shards,
        mesh=mesh,
        in_specs=placed,
        out_specs=(P("by", "bx"), P("by", "bx")),
        check_vma=False,
    )
```

```python
import jax
import jax.numpy as jnp
from jax import lax
from jax.experimental import pallas as pl
from jax.experimental.pallas import tpu as pltpu
from jax.sharding import PartitionSpec as P

ITERS = 4
VISCOSITY = 0.05
IMPLICIT = 0.05

ROWS = 8
PAD = 8
LANES = 128
REACH = 3
DEEP = ITERS
EDGE = ITERS + 1

STEP = 8
MIX_UNROLL = 17
SPREAD_UNROLL = 11
WIDE = 17
WIDE_INNER = 8


def message_rows(levels):
    forcing_at = REACH * levels
    count_at = forcing_at + DEEP
    pressure_at = count_at + EDGE
    total = pressure_at + EDGE
    return forcing_at, count_at, pressure_at, -(-total // 8) * 8


def lane_index():
    return lax.broadcasted_iota(jnp.int32, (STEP, LANES), 1)


def turn(value, by):
    return pltpu.roll(value, by % LANES, 1)


def neighbours(tiles, lane, by=1):
    count = len(tiles)
    back = [None if t is None else turn(t, -by) for t in tiles]
    forth = [None if t is None else turn(t, by) for t in tiles]

    def pick(mask, other, own):
        if other is None and own is None:
            return None
        zero = jnp.zeros((STEP, LANES), jnp.float32)
        return jnp.where(mask, zero if other is None else other, zero if own is None else own)

    east = [pick(lane >= LANES - by, back[(i + 1) % count], back[i]) for i in range(count)]
    west = [pick(lane < by, forth[i - 1], forth[i]) for i in range(count)]
    return east, west


def forcing_kernel(
    thick, fields, south, north, count, old, part, depth, guess, to_east, to_west,
    block, mixed, wet, pack, edges, arrivals,
):
    level = pl.program_id(0)
    levels = pl.num_programs(0)
    static_levels = fields.shape[1]
    height, width = count.shape
    tiles = width // LANES
    ext = height + 2 * ROWS
    base = PAD + ROWS
    forcing_at = message_rows(static_levels)[0]
    lane = lane_index()
    cols = [pl.ds(t * LANES, LANES) for t in range(tiles)]
    both = range(tiles + 1)

    def arrival(at, t):
        return pltpu.make_async_copy(
            fields.at[:, at, :, cols[t]],
            block.at[at, :, t, pl.ds(base, height), :],
            arrivals.at[at, t],
        )

    @pl.when(level == 0)
    def _():
        for at in range(static_levels):
            for t in range(tiles):
                arrival(at, t).start()

    def extended(e, lower, middle, upper):
        if e < ROWS:
            return lower
        if e >= ROWS + height:
            return upper
        return middle(e - ROWS)

    def sweep(body, strips, unroll):
        lax.fori_loop(0, strips, lambda i, c: (body(i), c)[1], 0, unroll=unroll)

    @pl.when(level == 0)
    def _():
        for buf in (mixed, depth, guess):
            for at in (0, PAD + ext):
                buf[:, at : at + PAD, :] = jnp.zeros((buf.shape[0], PAD, LANES), jnp.float32)
        part[...] = jnp.zeros_like(part)
        pack[...] = jnp.zeros_like(pack)
        edges[...] = jnp.zeros_like(edges)
        for t, c in enumerate(cols):
            wet[t, :ROWS, :] = south[3 * static_levels, :, c]
            wet[t, ROWS : ROWS + height, :] = count[:, c].astype(jnp.float32)
            wet[t, ROWS + height :, :] = north[3 * static_levels, :, c]

    zonal, merid, baro = (block.at[level, f] for f in range(3))
    for f, buf in enumerate((zonal, merid, baro)):
        for t, c in enumerate(cols):
            buf[t, :PAD, :] = jnp.zeros((PAD, LANES), jnp.float32)
            buf[t, PAD:base, :] = south[f * static_levels + level, :, c]
            buf[t, base + height : PAD + ext, :] = north[f * static_levels + level, :, c]
            buf[t, PAD + ext :, :] = jnp.zeros((PAD, LANES), jnp.float32)
    for t in range(tiles):
        arrival(level, t).wait()

    def near(i, by=0):
        return pl.ds(PAD + i * STEP + by, STEP)

    def mix(i):
        east, west = neighbours([zonal[t, near(i), :] for t in range(tiles)] + [None], lane)
        for t in both:
            value = east[t] - west[t]
            if t < tiles:
                value += merid[t, near(i, 1), :] - merid[t, near(i, -1), :]
            mixed[t, near(i), :] = value

    sweep(mix, ext // STEP, MIX_UNROLL)
    thickness = thick[level]
    level_number = level.astype(jnp.float32)

    def spread(i):
        rows = pl.ds(ROWS - DEEP + i * STEP, STEP)
        near = lambda i, by=0: pl.ds(PAD + ROWS - DEEP + i * STEP + by, STEP)
        far, once, still = [], [], []
        for t in both:
            own = mixed[t, near(i), :]
            beside = mixed[t, near(i, 1), :] + mixed[t, near(i, -1), :]
            beyond = mixed[t, near(i, 2), :] + mixed[t, near(i, -2), :]
            once.append(2.0 * beside - 8.0 * own)
            still.append(beyond - 8.0 * beside + 20.0 * own)
            if t < tiles:
                pressure = 10.0 * baro[t, near(i), :]
                around = baro[t, near(i, 2), :] + baro[t, near(i, -2), :]
                own = own + pressure
                still[t] += 10.0 * around - 4.0 * pressure
            far.append(own)
        count_of = len(far)
        back = [turn(v, -1) for v in far]
        forth = [turn(v, 1) for v in far]
        last, first = lane == LANES - 1, lane == 0
        easts = [
            once[t] + jnp.where(last, back[(t + 1) % count_of], back[t]) for t in both
        ]
        wests = [once[t] + jnp.where(first, forth[t - 1], forth[t]) for t in both]
        back = [turn(v, -1) for v in easts]
        forth = [turn(v, 1) for v in wests]
        for t in both:
            total = still[t] + (
                jnp.where(last, back[(t + 1) % count_of], back[t])
                + jnp.where(first, forth[t - 1], forth[t])
            )
            if t < tiles:
                weight = jnp.where(wet[t, rows, :] > level_number, thickness, 0.0)
                part[t, rows, :] += weight * total
            else:
                pack[rows, :] += pltpu.roll(total, 8 * level + REACH, 1)

    sweep(spread, (height + 2 * DEEP) // STEP, SPREAD_UNROLL)

    @pl.when(level == levels - 1)
    def _():
        scale = -0.5 * VISCOSITY
        for e in range(0, ext, STEP):
            r = e + PAD
            begin = []
            for t, c in enumerate(cols):
                pressure = extended(
                    e,
                    south[3 * static_levels + 1, :, c],
                    lambda o: old[o : o + STEP, c],
                    north[3 * static_levels + 1, :, c],
                )
                counts = wet[t, e : e + STEP, :]
                deep = sum(
                    jnp.where(counts > float(k), thick[k], 0.0) for k in range(static_levels)
                )
                depth[t, r : r + STEP, :] = deep
                begin.append(jnp.where(counts > 0.0, pressure, 0.0))
                guess[t, r : r + STEP, :] = begin[t]
                part[t, e : e + STEP, :] *= scale
            tile = None
            for t, inner, start in ((tiles - 1, True, 0), (0, False, LANES // 2)):
                at = start
                for piece, size in (
                    (part[t, e : e + STEP, :], DEEP),
                    (wet[t, e : e + STEP, :], EDGE),
                    (begin[t], EDGE),
                ):
                    moved = turn(piece, at + size if inner else at)
                    inside = (lane >= at) & (lane < at + size)
                    tile = jnp.where(inside, moved, 0.0 if tile is None else tile)
                    at += size
            edges[e : e + STEP, :] = tile
        size = DEEP + 2 * EDGE
        for message in (to_east, to_west):
            message[...] = jnp.zeros_like(message)
        for at in range(0, to_east.shape[1], LANES):
            span = slice(at, at + LANES)
            turned = scale * jnp.transpose(pack[span, :])
            for k in range(static_levels):
                mine = slice(REACH * k, REACH * k + REACH)
                to_west[mine, span] = turned[8 * k : 8 * k + REACH, :]
                to_east[mine, span] = turned[8 * k + REACH : 8 * k + 2 * REACH, :]
            turned = jnp.transpose(edges[span, :])
            to_east[forcing_at : forcing_at + size, span] = turned[:size, :]
            to_west[forcing_at : forcing_at + size, span] = turned[
                LANES // 2 : LANES // 2 + size, :
            ]


def solve_kernel(
    thick, part, depth, guess, to_east, to_west, from_west, from_east,
    bases, diag, moments,
    turned, fix, halo_part, halo_depth, halo_guess, half, half_w, inverse, vec_e, vec_w, sums,
):
    tiles, ext, _ = part.shape
    height = ext - 2 * ROWS
    levels = thick.shape[0]
    forcing_at, count_at, pressure_at, _ = message_rows(levels)
    lane = lane_index()

    def weights(counts):
        return [jnp.where(counts > float(k), thick[k], 0.0) for k in range(levels)]

    def weighted(counts, message):
        total = None
        for k, weight in enumerate(weights(counts)):
            term = weight * message[REACH * k : REACH * k + REACH, :]
            total = term if total is None else total + term
        return total

    def rows(message, at, size):
        return message[at : at + size, :]

    skip = EDGE - REACH
    turned[...] = jnp.zeros_like(turned)
    turned[0:DEEP, :] = rows(from_east, forcing_at, DEEP)
    turned[0:REACH, :] += weighted(rows(from_east, count_at, REACH), to_east)
    turned[LANES - DEEP : LANES, :] = rows(from_west, forcing_at, DEEP)
    turned[LANES - REACH : LANES, :] += weighted(rows(from_west, count_at + skip, REACH), to_west)
    turned[40 : 40 + EDGE, :] = sum(weights(rows(from_east, count_at, EDGE)))
    turned[40 - EDGE : 40, :] = sum(weights(rows(from_west, count_at, EDGE)))
    turned[60 : 60 + EDGE, :] = rows(from_east, pressure_at, EDGE)
    turned[60 - EDGE : 60, :] = rows(from_west, pressure_at, EDGE)
    turned[80 : 80 + REACH, :] = weighted(rows(to_west, count_at, REACH), from_west)
    turned[80 - REACH : 80, :] = weighted(rows(to_east, count_at + skip, REACH), from_east)

    for buf in (halo_depth, halo_guess):
        for at in (0, PAD + ext):
            buf[at : at + PAD, :] = jnp.zeros((PAD, LANES), jnp.float32)
    for at in (0, PAD + ext):
        for buf in (half, half_w):
            buf[:, at : at + PAD, :] = jnp.zeros((tiles + 1, PAD, LANES), jnp.float32)
        for buf in (vec_e, vec_w):
            buf[:, :, at : at + PAD, :] = jnp.zeros((2, tiles + 1, PAD, LANES), jnp.float32)
    near = (lane < EDGE) | (lane >= LANES - EDGE)
    close = (lane < DEEP) | (lane >= LANES - DEEP)
    for at in range(0, ext, LANES):
        block = jnp.transpose(turned[:, at : at + LANES])
        for e in range(at, min(at + LANES, ext), STEP):
            r = e + PAD
            tile = block[e - at : e - at + STEP, :]
            halo_depth[r : r + STEP, :] = jnp.where(near, turn(tile, -40), 0.0)
            halo_guess[r : r + STEP, :] = jnp.where(near, turn(tile, -60), 0.0)
            halo_part[e : e + STEP, :] = jnp.where(close, tile, 0.0)
            fix[e : e + STEP, :] = turn(tile, -80)

    def sweep(body, strips, unroll, first=0, stride=1, carry=0):
        step = lambda i, c: body(first + stride * i, c)
        return lax.fori_loop(0, strips, step, carry, unroll=unroll)

    def span(i, by=0):
        return pl.ds(PAD + i * STEP + by, STEP)

    def strip(i):
        return pl.ds(pl.multiple_of(i * STEP, STEP), STEP)

    def read(main, halo, rows):
        return [main[t, rows, :] for t in range(tiles)] + [halo[rows, :]]

    both = range(tiles + 1)
    inner = height // STEP
    above = ROWS // STEP

    def put_beside(values, slot, i):
        east, west = neighbours(values, lane)
        for t in both:
            vec_e[slot, t, span(i), :] = east[t]
            vec_w[slot, t, span(i), :] = west[t]

    def prepare(i, c):
        low = [
            jnp.minimum(a, b)
            for a, b in zip(
                read(depth, halo_depth, span(i)), read(depth, halo_depth, span(i, 1))
            )
        ]
        east, _ = neighbours(low, lane)
        corner = [0.5 * jnp.minimum(a, b) for a, b in zip(low, east)]
        _, west = neighbours(corner, lane)
        for t in both:
            half[t, span(i), :] = corner[t]
            half_w[t, span(i), :] = west[t]
        put_beside(read(guess, halo_guess, span(i)), 0, i)
        return c

    sweep(prepare, ext // STEP, WIDE)

    def around(slot, t, i):
        return (
            (half[t, span(i), :], vec_e[slot, t, span(i, 1), :]),
            (half_w[t, span(i), :], vec_w[slot, t, span(i, 1), :]),
            (half[t, span(i, -1), :], vec_e[slot, t, span(i, -1), :]),
            (half_w[t, span(i, -1), :], vec_w[slot, t, span(i, -1), :]),
        )

    def begin(inside):
        def body(i, c):
            here = read(guess, halo_guess, span(i))
            wide = read(depth, halo_depth, span(i))
            fixes = fix[strip(i), :]
            values = []
            for t in both:
                (ch, ne), (chw, nw), (ch_s, se), (chw_s, sw) = around(0, t, i)
                diagonal = IMPLICIT + ((ch + chw) + (ch_s + chw_s))
                inv = 1.0 / diagonal
                inverse[t, strip(i), :] = inv
                image = IMPLICIT * here[t] + (
                    (ch * (here[t] - ne) + chw * (here[t] - nw))
                    + (ch_s * (here[t] - se) + chw_s * (here[t] - sw))
                )
                total = halo_part[strip(i), :] if t == tiles else part[t, strip(i), :]
                if t == 0:
                    total += jnp.where(lane < REACH, fixes, 0.0)
                if t == tiles - 1:
                    total += jnp.where(lane >= LANES - REACH, fixes, 0.0)
                side = jnp.where(wide[t] > 0.0, total + IMPLICIT * here[t], 0.0)
                values.append((side - image) * inv)
                if inside and t < tiles:
                    bases[0, t, strip(i - above), :] = values[t]
                    diag[t, strip(i - above), :] = diagonal
            put_beside(values, 1, i)
            return c

        return body

    sweep(begin(True), inner, WIDE_INNER, above)
    sweep(begin(False), 2, 2, 0, above + inner)

    zero = jnp.zeros((STEP, LANES), jnp.float32)

    def power(j, c):
        source, target = lax.rem(j + 1, 2), lax.rem(j, 2)

        def apply(inside):
            def body(i, carry):
                even, odd = carry
                values = []
                for t in both:
                    (ch, ne), (chw, nw), (ch_s, se), (chw_s, sw) = around(source, t, i)
                    value = inverse[t, strip(i), :] * (
                        (ch * ne + chw * nw) + (ch_s * se + chw_s * sw)
                    )
                    values.append(value)
                    if inside and t < tiles:
                        now = bases[j, t, strip(i - above), :]
                        scaled = diag[t, strip(i - above), :] * now
                        even = even + scaled * now
                        odd = odd + scaled * value
                        bases[j + 1, t, strip(i - above), :] = value
                put_beside(values, target, i)
                return even, odd

            return body

        even, odd = sweep(apply(True), inner, WIDE_INNER, above, 1, (zero, zero))
        sweep(apply(False), 2, 2, 0, above + inner, (zero, zero))
        sums[2 * j] = even
        sums[2 * j + 1] = odd
        return c

    lax.fori_loop(0, ITERS, power, 0)
    lane_row = lax.broadcasted_iota(jnp.int32, (1, LANES), 1)
    found = jnp.zeros((1, LANES), jnp.float32)
    for m in range(2 * ITERS):
        found = jnp.where(lane_row == m, jnp.sum(sums[m]), found)
    for d in range(moments.shape[0]):
        moments[d] = found


def combine_kernel(moments, guess, bases, diag, pressure, residual):
    height, width = pressure.shape
    total = jnp.sum(moments[...], axis=0)
    h = [jnp.broadcast_to(total[:, m : m + 1], (STEP, LANES)) for m in range(2 * ITERS)]
    one, zero = jnp.ones((STEP, LANES), jnp.float32), None

    def plus(a, b):
        return b if a is None else a if b is None else a + b

    def times(a, b):
        return None if a is None or b is None else a * b

    def minus_n(poly):
        moved = [zero] + list(poly)
        return [
            a if b is None else (-b if a is None else a - b)
            for a, b in zip(list(poly) + [zero], moved)
        ]

    def inner(left, right):
        total = None
        for i, a in enumerate(left):
            part = None
            for j, b in enumerate(right):
                part = plus(part, times(b, h[i + j]))
            total = plus(total, times(a, part))
        return total

    rest, direction, answer = [one], [one], []
    norm = h[0]
    for iteration in range(ITERS):
        image = minus_n(direction)
        alpha = norm / inner(direction, image)
        answer = [
            plus(answer[i] if i < len(answer) else None, alpha * c)
            for i, c in enumerate(direction)
        ]
        rest = [
            plus(rest[i] if i < len(rest) else None, -(alpha * c)) for i, c in enumerate(image)
        ]
        if iteration + 1 < ITERS:
            following = inner(rest, rest)
            ratio = following / norm
            direction = [
                plus(c, ratio * direction[i] if i < len(direction) else None)
                for i, c in enumerate(rest)
            ]
            norm = following
    for t in range(width // LANES):
        for o in range(0, height, STEP):
            vecs = [bases[b, t, o : o + STEP, :] for b in range(ITERS + 1)]
            moved = sum(c * v for c, v in zip(answer, vecs))
            left = sum(c * v for c, v in zip(rest, vecs))
            at = PAD + ROWS + o
            cols = pl.ds(t * LANES, LANES)
            pressure[o : o + STEP, cols] = guess[t, at : at + STEP, :] + moved
            residual[o : o + STEP, cols] = diag[t, o : o + STEP, :] * left


def shift(value, axis, by):
    size = lax.axis_size(axis)
    return lax.ppermute(value, axis, [(i, (i + by) % size) for i in range(size)])


def shards(fields, level_count, thickness, old_pressure):
    levels, height, width = fields.shape[1:]
    ext, tall = height + 2 * ROWS, height + LANES
    f32 = jnp.float32

    def edge(at):
        pick = lambda a: lax.slice_in_dim(a, at, at + ROWS, axis=a.ndim - 2)
        flat = pick(fields).reshape(3 * levels, ROWS, width)
        return jnp.concatenate(
            [flat, pick(level_count).astype(f32)[None], pick(old_pressure)[None]], axis=0
        )

    south = shift(edge(height - ROWS), "by", 1)
    north = shift(edge(0), "by", -1)

    message = message_rows(levels)[3]
    tiles, padded = width // LANES, ext + 2 * PAD
    smem = pl.BlockSpec(memory_space=pltpu.SMEM)
    vmem = pl.BlockSpec(memory_space=pltpu.VMEM)
    whole = lambda *dims: pl.BlockSpec(dims, lambda k: (0,) * len(dims))
    hbm = pl.BlockSpec(memory_space=pl.ANY)
    halo = whole(3 * levels + 2, ROWS, width)
    shaped = lambda *dims: jax.ShapeDtypeStruct(dims, f32)
    scratch = lambda *dims: pltpu.VMEM(dims, f32)
    main = (tiles, ext, LANES)
    loose = (tiles, padded, LANES)
    results = (main, loose, loose, (message, tall), (message, tall))
    part, depth, guess, to_east, to_west = pl.pallas_call(
        forcing_kernel,
        grid=(levels,),
        in_specs=[
            smem,
            hbm, halo, halo,
            whole(height, width), whole(height, width),
        ],
        out_specs=[whole(*dims) for dims in results],
        out_shape=[shaped(*dims) for dims in results],
        scratch_shapes=[
            scratch(levels, 3, *loose),
            scratch(tiles + 1, padded, LANES),
            scratch(*main),
            scratch(tall, LANES),
            scratch(tall, LANES),
            pltpu.SemaphoreType.DMA((levels, tiles)),
        ],
        name="forcing",
    )(thickness, fields, south, north, level_count, old_pressure)

    from_west = shift(to_east, "bx", 1)
    from_east = shift(to_west, "bx", -1)

    devices = lax.axis_size("by") * lax.axis_size("bx")
    bases, diag, moments = pl.pallas_call(
        solve_kernel,
        in_specs=[smem] + [vmem] * 7,
        out_specs=[vmem] * 3,
        out_shape=[
            shaped(ITERS + 1, tiles, height, LANES),
            shaped(tiles, height, LANES),
            shaped(devices, 1, LANES),
        ],
        scratch_shapes=[scratch(LANES, tall), scratch(ext, LANES), scratch(ext, LANES)]
        + [scratch(padded, LANES)] * 2
        + [scratch(tiles + 1, padded, LANES)] * 2
        + [scratch(tiles + 1, ext, LANES)]
        + [scratch(2, tiles + 1, padded, LANES)] * 2
        + [scratch(2 * ITERS, STEP, LANES)],
        name="krylov",
    )(thickness, part, depth, guess, to_east, to_west, from_west, from_east)

    moments = lax.all_to_all(moments, ("by", "bx"), split_axis=0, concat_axis=0, tiled=True)
    return tuple(
        pl.pallas_call(
            combine_kernel,
            in_specs=[vmem] * 4,
            out_specs=[vmem] * 2,
            out_shape=[shaped(height, width)] * 2,
            name="combine",
        )(moments, guess, bases, diag)
    )


def solution(mesh):
    placed = (P(None, None, "by", "bx"), P("by", "bx"), P(), P("by", "bx"))
    return jax.shard_map(
        shards,
        mesh=mesh,
        in_specs=placed,
        out_specs=(P("by", "bx"), P("by", "bx")),
        check_vma=False,
    )
```

```python
import jax
import jax.numpy as jnp
from jax import lax
from jax.experimental import pallas as pl
from jax.experimental.pallas import tpu as pltpu
from jax.sharding import PartitionSpec as P

ITERS = 4
VISCOSITY = 0.05
IMPLICIT = 0.05

ROWS = 8
PAD = 8
LANES = 128
REACH = 3
DEEP = ITERS
EDGE = ITERS + 1

STEP = 8
GRANT = 16 * 2**20
MIX_UNROLL = 17
SPREAD_UNROLL = 11
WIDE = 17
WIDE_INNER = 16


def message_rows(levels):
    forcing_at = REACH * levels
    count_at = forcing_at + DEEP
    pressure_at = count_at + EDGE
    total = pressure_at + EDGE
    return forcing_at, count_at, pressure_at, -(-total // 8) * 8


def lane_index():
    return lax.broadcasted_iota(jnp.int32, (STEP, LANES), 1)


def turn(value, by):
    return pltpu.roll(value, by % LANES, 1)


def neighbours(tiles, lane, by=1):
    count = len(tiles)
    back = [None if t is None else turn(t, -by) for t in tiles]
    forth = [None if t is None else turn(t, by) for t in tiles]

    def pick(mask, other, own):
        if other is None and own is None:
            return None
        zero = jnp.zeros((STEP, LANES), jnp.float32)
        return jnp.where(mask, zero if other is None else other, zero if own is None else own)

    east = [pick(lane >= LANES - by, back[(i + 1) % count], back[i]) for i in range(count)]
    west = [pick(lane < by, forth[i - 1], forth[i]) for i in range(count)]
    return east, west


def forcing_kernel(
    thick, fields, south, north, count, old, part, depth, guess, to_east, to_west,
    block, mixed, wet, pack, edges, arrivals,
):
    level = pl.program_id(0)
    levels = pl.num_programs(0)
    static_levels = fields.shape[1]
    height, width = count.shape
    tiles = width // LANES
    ext = height + 2 * ROWS
    base = PAD + ROWS
    forcing_at = message_rows(static_levels)[0]
    lane = lane_index()
    cols = [pl.ds(t * LANES, LANES) for t in range(tiles)]
    both = range(tiles + 1)

    def arrival(at, t):
        return pltpu.make_async_copy(
            fields.at[:, at, :, cols[t]],
            block.at[at, :, t, pl.ds(base, height), :],
            arrivals.at[at, t],
        )

    @pl.when(level == 0)
    def _():
        for at in range(static_levels):
            for t in range(tiles):
                arrival(at, t).start()

    def extended(e, lower, middle, upper):
        if e < ROWS:
            return lower
        if e >= ROWS + height:
            return upper
        return middle(e - ROWS)

    def sweep(body, strips, unroll):
        lax.fori_loop(0, strips, lambda i, c: (body(i), c)[1], 0, unroll=unroll)

    @pl.when(level == 0)
    def _():
        for buf in (mixed, depth, guess):
            for at in (0, PAD + ext):
                buf[:, at : at + PAD, :] = jnp.zeros((buf.shape[0], PAD, LANES), jnp.float32)
        part[...] = jnp.zeros_like(part)
        pack[...] = jnp.zeros_like(pack)
        edges[...] = jnp.zeros_like(edges)
        for t, c in enumerate(cols):
            wet[t, :ROWS, :] = south[3 * static_levels, :, c]
            wet[t, ROWS : ROWS + height, :] = count[:, c].astype(jnp.float32)
            wet[t, ROWS + height :, :] = north[3 * static_levels, :, c]

    zonal, merid, baro = (block.at[level, f] for f in range(3))
    for f, buf in enumerate((zonal, merid, baro)):
        for t, c in enumerate(cols):
            buf[t, :PAD, :] = jnp.zeros((PAD, LANES), jnp.float32)
            buf[t, PAD:base, :] = south[f * static_levels + level, :, c]
            buf[t, base + height : PAD + ext, :] = north[f * static_levels + level, :, c]
            buf[t, PAD + ext :, :] = jnp.zeros((PAD, LANES), jnp.float32)
    for t in range(tiles):
        arrival(level, t).wait()

    def near(i, by=0):
        return pl.ds(PAD + i * STEP + by, STEP)

    def mix(i):
        east, west = neighbours([zonal[t, near(i), :] for t in range(tiles)] + [None], lane)
        for t in both:
            value = east[t] - west[t]
            if t < tiles:
                value += merid[t, near(i, 1), :] - merid[t, near(i, -1), :]
            mixed[t, near(i), :] = value

    sweep(mix, ext // STEP, MIX_UNROLL)
    thickness = thick[level]
    level_number = level.astype(jnp.float32)

    def spread(i):
        rows = pl.ds(ROWS - DEEP + i * STEP, STEP)
        near = lambda i, by=0: pl.ds(PAD + ROWS - DEEP + i * STEP + by, STEP)
        far, once, still = [], [], []
        for t in both:
            own = mixed[t, near(i), :]
            beside = mixed[t, near(i, 1), :] + mixed[t, near(i, -1), :]
            beyond = mixed[t, near(i, 2), :] + mixed[t, near(i, -2), :]
            once.append(2.0 * beside - 8.0 * own)
            still.append(beyond - 8.0 * beside + 20.0 * own)
            if t < tiles:
                pressure = 10.0 * baro[t, near(i), :]
                around = baro[t, near(i, 2), :] + baro[t, near(i, -2), :]
                own = own + pressure
                still[t] += 10.0 * around - 4.0 * pressure
            far.append(own)
        count_of = len(far)
        back = [turn(v, -1) for v in far]
        forth = [turn(v, 1) for v in far]
        last, first = lane == LANES - 1, lane == 0
        easts = [
            once[t] + jnp.where(last, back[(t + 1) % count_of], back[t]) for t in both
        ]
        wests = [once[t] + jnp.where(first, forth[t - 1], forth[t]) for t in both]
        back = [turn(v, -1) for v in easts]
        forth = [turn(v, 1) for v in wests]
        for t in both:
            total = still[t] + (
                jnp.where(last, back[(t + 1) % count_of], back[t])
                + jnp.where(first, forth[t - 1], forth[t])
            )
            if t < tiles:
                weight = jnp.where(wet[t, rows, :] > level_number, thickness, 0.0)
                part[t, rows, :] += weight * total
            else:
                pack[rows, :] += pltpu.roll(total, 8 * level + REACH, 1)

    sweep(spread, (height + 2 * DEEP) // STEP, SPREAD_UNROLL)

    @pl.when(level == levels - 1)
    def _():
        scale = -0.5 * VISCOSITY
        for e in range(0, ext, STEP):
            r = e + PAD
            begin = []
            for t, c in enumerate(cols):
                pressure = extended(
                    e,
                    south[3 * static_levels + 1, :, c],
                    lambda o: old[o : o + STEP, c],
                    north[3 * static_levels + 1, :, c],
                )
                counts = wet[t, e : e + STEP, :]
                deep = sum(
                    jnp.where(counts > float(k), thick[k], 0.0) for k in range(static_levels)
                )
                depth[t, r : r + STEP, :] = deep
                begin.append(jnp.where(counts > 0.0, pressure, 0.0))
                guess[t, r : r + STEP, :] = begin[t]
                part[t, e : e + STEP, :] *= scale
            tile = None
            for t, inner, start in ((tiles - 1, True, 0), (0, False, LANES // 2)):
                at = start
                for piece, size in (
                    (part[t, e : e + STEP, :], DEEP),
                    (wet[t, e : e + STEP, :], EDGE),
                    (begin[t], EDGE),
                ):
                    moved = turn(piece, at + size if inner else at)
                    inside = (lane >= at) & (lane < at + size)
                    tile = jnp.where(inside, moved, 0.0 if tile is None else tile)
                    at += size
            edges[e : e + STEP, :] = tile
        size = DEEP + 2 * EDGE
        for message in (to_east, to_west):
            message[...] = jnp.zeros_like(message)
        for at in range(0, to_east.shape[1], LANES):
            span = slice(at, at + LANES)
            turned = scale * jnp.transpose(pack[span, :])
            for k in range(static_levels):
                mine = slice(REACH * k, REACH * k + REACH)
                to_west[mine, span] = turned[8 * k : 8 * k + REACH, :]
                to_east[mine, span] = turned[8 * k + REACH : 8 * k + 2 * REACH, :]
            turned = jnp.transpose(edges[span, :])
            to_east[forcing_at : forcing_at + size, span] = turned[:size, :]
            to_west[forcing_at : forcing_at + size, span] = turned[
                LANES // 2 : LANES // 2 + size, :
            ]


def solve_kernel(
    thick, part, depth, guess, to_east, to_west, from_west, from_east,
    base0, base1, base2, base3, base4, diag, moments,
    turned, fix, halo_part, halo_depth, halo_guess, half, half_w, inverse, even_e, even_w, odd_e, odd_w,
):
    tiles, ext, _ = part.shape
    height = ext - 2 * ROWS
    levels = thick.shape[0]
    forcing_at, count_at, pressure_at, _ = message_rows(levels)
    lane = lane_index()

    def weights(counts):
        return [jnp.where(counts > float(k), thick[k], 0.0) for k in range(levels)]

    def weighted(counts, message):
        total = None
        for k, weight in enumerate(weights(counts)):
            term = weight * message[REACH * k : REACH * k + REACH, :]
            total = term if total is None else total + term
        return total

    def rows(message, at, size):
        return message[at : at + size, :]

    skip = EDGE - REACH
    turned[...] = jnp.zeros_like(turned)
    turned[0:DEEP, :] = rows(from_east, forcing_at, DEEP)
    turned[0:REACH, :] += weighted(rows(from_east, count_at, REACH), to_east)
    turned[LANES - DEEP : LANES, :] = rows(from_west, forcing_at, DEEP)
    turned[LANES - REACH : LANES, :] += weighted(rows(from_west, count_at + skip, REACH), to_west)
    turned[40 : 40 + EDGE, :] = sum(weights(rows(from_east, count_at, EDGE)))
    turned[40 - EDGE : 40, :] = sum(weights(rows(from_west, count_at, EDGE)))
    turned[60 : 60 + EDGE, :] = rows(from_east, pressure_at, EDGE)
    turned[60 - EDGE : 60, :] = rows(from_west, pressure_at, EDGE)
    turned[80 : 80 + REACH, :] = weighted(rows(to_west, count_at, REACH), from_west)
    turned[80 - REACH : 80, :] = weighted(rows(to_east, count_at + skip, REACH), from_east)

    for buf in (halo_depth, halo_guess):
        for at in (0, PAD + ext):
            buf[at : at + PAD, :] = jnp.zeros((PAD, LANES), jnp.float32)
    for at in (0, PAD + ext):
        for buf in (half, half_w, even_e, even_w, odd_e, odd_w):
            buf[:, at : at + PAD, :] = jnp.zeros((tiles + 1, PAD, LANES), jnp.float32)
    near = (lane < EDGE) | (lane >= LANES - EDGE)
    close = (lane < DEEP) | (lane >= LANES - DEEP)
    for at in range(0, ext, LANES):
        block = jnp.transpose(turned[:, at : at + LANES])
        for e in range(at, min(at + LANES, ext), STEP):
            r = e + PAD
            tile = block[e - at : e - at + STEP, :]
            halo_depth[r : r + STEP, :] = jnp.where(near, turn(tile, -40), 0.0)
            halo_guess[r : r + STEP, :] = jnp.where(near, turn(tile, -60), 0.0)
            halo_part[e : e + STEP, :] = jnp.where(close, tile, 0.0)
            fix[e : e + STEP, :] = turn(tile, -80)

    def sweep(body, strips, unroll, first=0, stride=1, carry=0):
        step = lambda i, c: body(first + stride * i, c)
        return lax.fori_loop(0, strips, step, carry, unroll=unroll)

    def span(i, by=0):
        return pl.ds(PAD + i * STEP + by, STEP)

    def strip(i):
        return pl.ds(pl.multiple_of(i * STEP, STEP), STEP)

    def read(main, halo, rows):
        return [main[t, rows, :] for t in range(tiles)] + [halo[rows, :]]

    shifted = ((even_e, even_w), (odd_e, odd_w))
    bases = (base0, base1, base2, base3, base4)
    both = range(tiles + 1)
    inner = height // STEP
    above = ROWS // STEP

    def put_beside(values, slot, i):
        east, west = neighbours(values, lane)
        for t in both:
            shifted[slot][0][t, span(i), :] = east[t]
            shifted[slot][1][t, span(i), :] = west[t]

    def prepare(i, c):
        low = [
            jnp.minimum(a, b)
            for a, b in zip(
                read(depth, halo_depth, span(i)), read(depth, halo_depth, span(i, 1))
            )
        ]
        east, _ = neighbours(low, lane)
        corner = [0.5 * jnp.minimum(a, b) for a, b in zip(low, east)]
        _, west = neighbours(corner, lane)
        for t in both:
            half[t, span(i), :] = corner[t]
            half_w[t, span(i), :] = west[t]
        put_beside(read(guess, halo_guess, span(i)), 0, i)
        return c

    sweep(prepare, ext // STEP, WIDE)

    def around(slot, t, i):
        vec_e, vec_w = shifted[slot]
        return (
            (half[t, span(i), :], vec_e[t, span(i, 1), :]),
            (half_w[t, span(i), :], vec_w[t, span(i, 1), :]),
            (half[t, span(i, -1), :], vec_e[t, span(i, -1), :]),
            (half_w[t, span(i, -1), :], vec_w[t, span(i, -1), :]),
        )

    def begin(inside):
        def body(i, c):
            here = read(guess, halo_guess, span(i))
            wide = read(depth, halo_depth, span(i))
            fixes = fix[strip(i), :]
            values = []
            for t in both:
                (ch, ne), (chw, nw), (ch_s, se), (chw_s, sw) = around(0, t, i)
                diagonal = IMPLICIT + ((ch + chw) + (ch_s + chw_s))
                inv = 1.0 / diagonal
                inverse[t, strip(i), :] = inv
                image = IMPLICIT * here[t] + (
                    (ch * (here[t] - ne) + chw * (here[t] - nw))
                    + (ch_s * (here[t] - se) + chw_s * (here[t] - sw))
                )
                total = halo_part[strip(i), :] if t == tiles else part[t, strip(i), :]
                if t == 0:
                    total += jnp.where(lane < REACH, fixes, 0.0)
                if t == tiles - 1:
                    total += jnp.where(lane >= LANES - REACH, fixes, 0.0)
                side = jnp.where(wide[t] > 0.0, total + IMPLICIT * here[t], 0.0)
                values.append((side - image) * inv)
                if inside and t < tiles:
                    base0[t, strip(i - above), :] = values[t]
                    diag[t, strip(i - above), :] = diagonal
            put_beside(values, 1, i)
            return c

        return body

    sweep(begin(True), inner, WIDE_INNER, above)
    sweep(begin(False), 2, 2, 0, above + inner)

    zero = jnp.zeros((STEP, LANES), jnp.float32)

    sums = []
    for j in range(ITERS):
        final = j + 1 == ITERS

        def apply(inside, j=j, final=final):
            def body(i, carry):
                even, odd = carry
                values = []
                for t in both:
                    if final and t == tiles:
                        continue
                    (ch, ne), (chw, nw), (ch_s, se), (chw_s, sw) = around((j + 1) % 2, t, i)
                    value = inverse[t, strip(i), :] * (
                        (ch * ne + chw * nw) + (ch_s * se + chw_s * sw)
                    )
                    values.append(value)
                    if inside and t < tiles:
                        now = bases[j][t, strip(i - above), :]
                        scaled = diag[t, strip(i - above), :] * now
                        even = even + scaled * now
                        odd = odd + scaled * value
                        bases[j + 1][t, strip(i - above), :] = value
                if not final:
                    put_beside(values, j % 2, i)
                return even, odd

            return body

        sums += sweep(apply(True), inner, WIDE_INNER, above, 1, (zero, zero))
        if not final:
            sweep(apply(False), 2, 2, 0, above + inner, (zero, zero))
    lane_row = lax.broadcasted_iota(jnp.int32, (1, LANES), 1)
    found = jnp.zeros((1, LANES), jnp.float32)
    for m in range(2 * ITERS):
        found = jnp.where(lane_row == m, jnp.sum(sums[m]), found)
    for d in range(moments.shape[0]):
        moments[d] = found


def combine_kernel(moments, guess, base0, base1, base2, base3, base4, diag, pressure, residual):
    height, width = pressure.shape
    total = jnp.sum(moments[...], axis=0)
    h = [jnp.broadcast_to(total[:, m : m + 1], (STEP, LANES)) for m in range(2 * ITERS)]
    one, zero = jnp.ones((STEP, LANES), jnp.float32), None

    def plus(a, b):
        return b if a is None else a if b is None else a + b

    def times(a, b):
        return None if a is None or b is None else a * b

    def minus_n(poly):
        moved = [zero] + list(poly)
        return [
            a if b is None else (-b if a is None else a - b)
            for a, b in zip(list(poly) + [zero], moved)
        ]

    def inner(left, right):
        total = None
        for i, a in enumerate(left):
            part = None
            for j, b in enumerate(right):
                part = plus(part, times(b, h[i + j]))
            total = plus(total, times(a, part))
        return total

    rest, direction, answer = [one], [one], []
    norm = h[0]
    for iteration in range(ITERS):
        image = minus_n(direction)
        alpha = norm / inner(direction, image)
        answer = [
            plus(answer[i] if i < len(answer) else None, alpha * c)
            for i, c in enumerate(direction)
        ]
        rest = [
            plus(rest[i] if i < len(rest) else None, -(alpha * c)) for i, c in enumerate(image)
        ]
        if iteration + 1 < ITERS:
            following = inner(rest, rest)
            ratio = following / norm
            direction = [
                plus(c, ratio * direction[i] if i < len(direction) else None)
                for i, c in enumerate(rest)
            ]
            norm = following
    bases = (base0, base1, base2, base3, base4)
    for t in range(width // LANES):
        for o in range(0, height, STEP):
            vecs = [b[t, o : o + STEP, :] for b in bases]
            moved = sum(c * v for c, v in zip(answer, vecs))
            left = sum(c * v for c, v in zip(rest, vecs))
            at = PAD + ROWS + o
            cols = pl.ds(t * LANES, LANES)
            pressure[o : o + STEP, cols] = guess[t, at : at + STEP, :] + moved
            residual[o : o + STEP, cols] = diag[t, o : o + STEP, :] * left


def shift(value, axis, by):
    size = lax.axis_size(axis)
    return lax.ppermute(value, axis, [(i, (i + by) % size) for i in range(size)])


def shards(fields, level_count, thickness, old_pressure):
    levels, height, width = fields.shape[1:]
    ext, tall = height + 2 * ROWS, height + LANES
    f32 = jnp.float32

    def edge(at):
        pick = lambda a: lax.slice_in_dim(a, at, at + ROWS, axis=a.ndim - 2)
        flat = pick(fields).reshape(3 * levels, ROWS, width)
        return jnp.concatenate(
            [flat, pick(level_count).astype(f32)[None], pick(old_pressure)[None]], axis=0
        )

    south = shift(edge(height - ROWS), "by", 1)
    north = shift(edge(0), "by", -1)

    message = message_rows(levels)[3]
    tiles, padded = width // LANES, ext + 2 * PAD
    smem = pl.BlockSpec(memory_space=pltpu.SMEM)
    vmem = pl.BlockSpec(memory_space=pltpu.VMEM)
    whole = lambda *dims: pl.BlockSpec(dims, lambda k: (0,) * len(dims))
    hbm = pl.BlockSpec(memory_space=pl.ANY)
    halo = whole(3 * levels + 2, ROWS, width)
    shaped = lambda *dims: jax.ShapeDtypeStruct(dims, f32)
    scratch = lambda *dims: pltpu.VMEM(dims, f32)
    main = (tiles, ext, LANES)
    loose = (tiles, padded, LANES)
    results = (main, loose, loose, (message, tall), (message, tall))
    part, depth, guess, to_east, to_west = pl.pallas_call(
        forcing_kernel,
        grid=(levels,),
        in_specs=[
            smem,
            hbm, halo, halo,
            whole(height, width), whole(height, width),
        ],
        out_specs=[whole(*dims) for dims in results],
        out_shape=[shaped(*dims) for dims in results],
        scratch_shapes=[
            scratch(levels, 3, *loose),
            scratch(tiles + 1, padded, LANES),
            scratch(*main),
            scratch(tall, LANES),
            scratch(tall, LANES),
            pltpu.SemaphoreType.DMA((levels, tiles)),
        ],
        compiler_params=pltpu.CompilerParams(vmem_limit_bytes=GRANT),
        name="forcing",
    )(thickness, fields, south, north, level_count, old_pressure)

    from_west = shift(to_east, "bx", 1)
    from_east = shift(to_west, "bx", -1)

    devices = lax.axis_size("by") * lax.axis_size("bx")
    *bases, diag, moments = pl.pallas_call(
        solve_kernel,
        in_specs=[smem] + [vmem] * 7,
        out_specs=[vmem] * (ITERS + 3),
        out_shape=[
            *[shaped(tiles, height, LANES)] * (ITERS + 2),
            shaped(devices, 1, LANES),
        ],
        scratch_shapes=[scratch(LANES, tall), scratch(ext, LANES), scratch(ext, LANES)]
        + [scratch(padded, LANES)] * 2
        + [scratch(tiles + 1, padded, LANES)] * 2
        + [scratch(tiles + 1, ext, LANES)]
        + [scratch(tiles + 1, padded, LANES)] * 4,
        compiler_params=pltpu.CompilerParams(vmem_limit_bytes=GRANT),
        name="krylov",
    )(thickness, part, depth, guess, to_east, to_west, from_west, from_east)

    moments = lax.all_to_all(moments, ("by", "bx"), split_axis=0, concat_axis=0, tiled=True)
    return tuple(
        pl.pallas_call(
            combine_kernel,
            in_specs=[vmem] * (ITERS + 4),
            out_specs=[vmem] * 2,
            out_shape=[shaped(height, width)] * 2,
            compiler_params=pltpu.CompilerParams(vmem_limit_bytes=GRANT),
            name="combine",
        )(moments, guess, *bases, diag)
    )


def solution(mesh):
    placed = (P(None, None, "by", "bx"), P("by", "bx"), P(), P("by", "bx"))
    return jax.shard_map(
        shards,
        mesh=mesh,
        in_specs=placed,
        out_specs=(P("by", "bx"), P("by", "bx")),
        check_vma=False,
    )
```

```python
import jax
import jax.numpy as jnp
from jax import lax
from jax.experimental import pallas as pl
from jax.experimental.pallas import tpu as pltpu
from jax.sharding import PartitionSpec as P

ITERS = 4
VISCOSITY = 0.05
IMPLICIT = 0.05

ROWS = 8
PAD = 8
LANES = 128
REACH = 3
DEEP = ITERS
EDGE = ITERS + 1

STEP = 8
GRANT = 16 * 2**20
INNER_GRANT = 52 * 2**20
MIX_UNROLL = 16
SPREAD_UNROLL = 10
WIDE = 17
WIDE_INNER = 16


def message_rows(levels):
    forcing_at = REACH * levels
    count_at = forcing_at + DEEP
    pressure_at = count_at + EDGE
    total = pressure_at + EDGE
    return forcing_at, count_at, pressure_at, -(-total // 8) * 8


def lane_index():
    return lax.broadcasted_iota(jnp.int32, (STEP, LANES), 1)


def turn(value, by):
    return pltpu.roll(value, by % LANES, 1)


def neighbours(tiles, lane, by=1):
    count = len(tiles)
    back = [None if t is None else turn(t, -by) for t in tiles]
    forth = [None if t is None else turn(t, by) for t in tiles]

    def pick(mask, other, own):
        if other is None and own is None:
            return None
        zero = jnp.zeros((STEP, LANES), jnp.float32)
        return jnp.where(mask, zero if other is None else other, zero if own is None else own)

    east = [pick(lane >= LANES - by, back[(i + 1) % count], back[i]) for i in range(count)]
    west = [pick(lane < by, forth[i - 1], forth[i]) for i in range(count)]
    return east, west


def mix_strip(zonal, merid, mixed, row, lane):
    tiles = zonal.shape[0]
    near = lambda by=0: pl.ds(row + by, STEP)
    east, west = neighbours([zonal[t, near(), :] for t in range(tiles)] + [None], lane)
    for t in range(tiles + 1):
        value = east[t] - west[t]
        if t < tiles:
            value += merid[t, near(1), :] - merid[t, near(-1), :]
        mixed[t, near(), :] = value


def spread_strip(baro, mixed, row, lane):
    tiles = baro.shape[0]
    both = range(tiles + 1)
    near = lambda by=0: pl.ds(row + by, STEP)
    far, once, still = [], [], []
    for t in both:
        own = mixed[t, near(), :]
        beside = mixed[t, near(1), :] + mixed[t, near(-1), :]
        beyond = mixed[t, near(2), :] + mixed[t, near(-2), :]
        once.append(2.0 * beside - 8.0 * own)
        still.append(beyond - 8.0 * beside + 20.0 * own)
        if t < tiles:
            pressure = 10.0 * baro[t, near(), :]
            around = baro[t, near(2), :] + baro[t, near(-2), :]
            own = own + pressure
            still[t] += 10.0 * around - 4.0 * pressure
        far.append(own)
    last, first = lane == LANES - 1, lane == 0
    ring = tiles + 1
    back = [turn(v, -1) for v in far]
    forth = [turn(v, 1) for v in far]
    easts = [once[t] + jnp.where(last, back[(t + 1) % ring], back[t]) for t in both]
    wests = [once[t] + jnp.where(first, forth[t - 1], forth[t]) for t in both]
    back = [turn(v, -1) for v in easts]
    forth = [turn(v, 1) for v in wests]
    return [
        still[t]
        + (
            jnp.where(last, back[(t + 1) % ring], back[t])
            + jnp.where(first, forth[t - 1], forth[t])
        )
        for t in both
    ]


def sweep(body, strips, unroll, carry=0, first=0, stride=1):
    step = lambda i, c: body(first + stride * i, c)
    return lax.fori_loop(0, strips, step, carry, unroll=unroll)


def lane_tiles(tiles):
    return [pl.ds(t * LANES, LANES) for t in range(tiles)]


def inner_kernel(thick, fields, count_hbm, part, pack, block, mixed, count, arrivals, others):
    level = pl.program_id(0)
    levels = fields.shape[1]
    tiles, height, _ = count.shape
    lane = lane_index()
    cols = lane_tiles(tiles)

    def arrival(at, t):
        return pltpu.make_async_copy(
            fields.at[:, at, :, cols[t]], block.at[at, :, t, pl.ds(PAD, height), :], arrivals.at[at, t]
        )

    counted = [
        pltpu.make_async_copy(count_hbm.at[:, cols[t]], count.at[t], others.at[t])
        for t in range(tiles)
    ]

    @pl.when(level == 0)
    def _():
        for t in range(tiles):
            arrival(0, t).start()
        for copy in counted:
            copy.start()
        for at in range(1, levels):
            for t in range(tiles):
                arrival(at, t).start()
        part[...] = jnp.zeros_like(part)
        pack[...] = jnp.zeros_like(pack)
        for copy in counted:
            copy.wait()

    for t in range(tiles):
        arrival(level, t).wait()
    zonal, merid, baro = (block.at[level, f] for f in range(3))
    thickness = thick[level]

    def mix(i, c):
        mix_strip(zonal, merid, mixed, PAD + i * STEP, lane)
        return c

    def spread(i, c):
        row = ROWS - DEEP + i * STEP
        total = spread_strip(baro, mixed, PAD + row, lane)
        rows = pl.ds(ROWS + row, STEP)
        for t in range(tiles):
            weight = jnp.where(count[t, pl.ds(row, STEP), :] > level, thickness, 0.0)
            part[t, rows, :] += weight * total[t]
        pack[rows, :] += pltpu.roll(total[tiles], 8 * level + REACH, 1)
        return c

    sweep(mix, height // STEP, MIX_UNROLL)
    strips = height // STEP - 1
    main = strips // SPREAD_UNROLL * SPREAD_UNROLL
    sweep(spread, main, SPREAD_UNROLL)
    for i in range(main, strips):
        spread(i, 0)


def edge_kernel(
    thick, fields, south, north, count_hbm, old_hbm, part_in, pack_in,
    part, depth, guess, to_east, to_west,
    pack, block, mixed, wet, edges, count, old, arrivals, others,
):
    levels = fields.shape[1]
    height, width = count.shape
    tiles = width // LANES
    ext = height + 2 * ROWS
    forcing_at = message_rows(levels)[0]
    lane = lane_index()
    cols = lane_tiles(tiles)

    copies = [
        pltpu.make_async_copy(count_hbm, count, others.at[0]),
        pltpu.make_async_copy(old_hbm, old, others.at[1]),
    ]
    for f in range(3):
        for t, c in enumerate(cols):
            for side, (here, there, halo, row) in enumerate(
                ((ROWS, 0, south, 0), (0, 2 * ROWS, north, height - 2 * ROWS))
            ):
                at = 4 * (f * tiles + t) + 2 * side
                group = block.at[side, f, :, t]
                copies += [
                    pltpu.make_async_copy(
                        fields.at[f, :, pl.ds(row, 2 * ROWS), c],
                        group.at[:, pl.ds(here, 2 * ROWS), :],
                        arrivals.at[at],
                    ),
                    pltpu.make_async_copy(
                        halo.at[pl.ds(f * levels, levels), :, c],
                        group.at[:, pl.ds(there, ROWS), :],
                        arrivals.at[at + 1],
                    ),
                ]
    for copy in copies:
        copy.start()
    low, high = slice(0, ROWS - DEEP), slice(ext - (ROWS - DEEP), ext)
    for buf in (depth, guess):
        for at in (0, PAD + ext):
            buf[:, at : at + PAD, :] = jnp.zeros((tiles, PAD, LANES), jnp.float32)
    inner = slice(2 * ROWS - DEEP, ext - (2 * ROWS - DEEP))
    part[:, inner, :] = part_in[:, inner, :]
    pack[inner, :] = pack_in[inner, :]
    for outer in (low, high, slice(ext, pack.shape[0])):
        if outer.start < ext:
            part[:, outer, :] = jnp.zeros((tiles, ROWS - DEEP, LANES), jnp.float32)
        pack[outer, :] = jnp.zeros((outer.stop - outer.start, LANES), jnp.float32)
    edges[ext:, :] = jnp.zeros((edges.shape[0] - ext, LANES), jnp.float32)
    for copy in copies:
        copy.wait()
    for t, c in enumerate(cols):
        wet[t, :ROWS, :] = south[3 * levels, :, c]
        wet[t, ROWS : ROWS + height, :] = count[:, c].astype(jnp.float32)
        wet[t, ROWS + height :, :] = north[3 * levels, :, c]

    plans = ((ROWS - DEEP, (2, 10)), (2 * ROWS - DEEP, (10, 14)))
    starts = (ROWS - DEEP, ext - (2 * ROWS - DEEP))

    def mix(k, c):
        for side, (_, rows) in enumerate(plans):
            for row in rows:
                mix_strip(block.at[side, 0, k], block.at[side, 1, k], mixed.at[side, k], row, lane)
        return c

    def spread(k, carry):
        found = []
        number, thickness = k.astype(jnp.float32), thick[k]
        for side, (row, _) in enumerate(plans):
            total = spread_strip(block.at[side, 2, k], mixed.at[side, k], row, lane)
            e = starts[side]
            for t in range(tiles):
                weight = jnp.where(wet[t, e : e + STEP, :] > number, thickness, 0.0)
                found.append(weight * total[t])
            found.append(pltpu.roll(total[tiles], 8 * k + REACH, 1))
        return tuple(a + b for a, b in zip(carry, found))

    sweep(mix, levels, 4)
    zero = jnp.zeros((STEP, LANES), jnp.float32)
    found = sweep(spread, levels, 4, (zero,) * (2 * (tiles + 1)))
    for side, e in enumerate(starts):
        for t in range(tiles):
            part[t, e : e + STEP, :] = found[side * (tiles + 1) + t]
        pack[e : e + STEP, :] = found[side * (tiles + 1) + tiles]

    scale = -0.5 * VISCOSITY
    for e in range(0, ext, STEP):
        r = e + PAD
        begin = []
        for t, c in enumerate(cols):
            if e < ROWS:
                pressure = south[3 * levels + 1, :, c]
            elif e >= ROWS + height:
                pressure = north[3 * levels + 1, :, c]
            else:
                pressure = old[e - ROWS : e - ROWS + STEP, c]
            counts = wet[t, e : e + STEP, :]
            depth[t, r : r + STEP, :] = sum(
                jnp.where(counts > float(k), thick[k], 0.0) for k in range(levels)
            )
            begin.append(jnp.where(counts > 0.0, pressure, 0.0))
            guess[t, r : r + STEP, :] = begin[t]
            part[t, e : e + STEP, :] *= scale
        tile = None
        for t, inside, start in ((tiles - 1, True, 0), (0, False, LANES // 2)):
            at = start
            for piece, size in (
                (part[t, e : e + STEP, :], DEEP),
                (wet[t, e : e + STEP, :], EDGE),
                (begin[t], EDGE),
            ):
                moved = turn(piece, at + size if inside else at)
                mask = (lane >= at) & (lane < at + size)
                tile = jnp.where(mask, moved, 0.0 if tile is None else tile)
                at += size
        edges[e : e + STEP, :] = tile
    size = DEEP + 2 * EDGE
    for message in (to_east, to_west):
        message[...] = jnp.zeros_like(message)
    for at in range(0, to_east.shape[1], LANES):
        span = slice(at, at + LANES)
        turned = scale * jnp.transpose(pack[span, :])
        for k in range(levels):
            mine = slice(REACH * k, REACH * k + REACH)
            to_west[mine, span] = turned[8 * k : 8 * k + REACH, :]
            to_east[mine, span] = turned[8 * k + REACH : 8 * k + 2 * REACH, :]
        turned = jnp.transpose(edges[span, :])
        to_east[forcing_at : forcing_at + size, span] = turned[:size, :]
        to_west[forcing_at : forcing_at + size, span] = turned[LANES // 2 : LANES // 2 + size, :]


def solve_kernel(
    thick, part, depth, guess, to_east, to_west, from_west, from_east,
    base0, base1, base2, base3, base4, diag, moments,
    turned, fix, halo_part, halo_depth, halo_guess, half, half_w, inverse, even_e, even_w, odd_e, odd_w,
):
    tiles, ext, _ = part.shape
    height = ext - 2 * ROWS
    levels = thick.shape[0]
    forcing_at, count_at, pressure_at, _ = message_rows(levels)
    lane = lane_index()

    def weights(counts):
        return [jnp.where(counts > float(k), thick[k], 0.0) for k in range(levels)]

    def weighted(counts, message):
        total = None
        for k, weight in enumerate(weights(counts)):
            term = weight * message[REACH * k : REACH * k + REACH, :]
            total = term if total is None else total + term
        return total

    def rows(message, at, size):
        return message[at : at + size, :]

    skip = EDGE - REACH
    turned[...] = jnp.zeros_like(turned)
    turned[0:DEEP, :] = rows(from_east, forcing_at, DEEP)
    turned[0:REACH, :] += weighted(rows(from_east, count_at, REACH), to_east)
    turned[LANES - DEEP : LANES, :] = rows(from_west, forcing_at, DEEP)
    turned[LANES - REACH : LANES, :] += weighted(rows(from_west, count_at + skip, REACH), to_west)
    turned[40 : 40 + EDGE, :] = sum(weights(rows(from_east, count_at, EDGE)))
    turned[40 - EDGE : 40, :] = sum(weights(rows(from_west, count_at, EDGE)))
    turned[60 : 60 + EDGE, :] = rows(from_east, pressure_at, EDGE)
    turned[60 - EDGE : 60, :] = rows(from_west, pressure_at, EDGE)
    turned[80 : 80 + REACH, :] = weighted(rows(to_west, count_at, REACH), from_west)
    turned[80 - REACH : 80, :] = weighted(rows(to_east, count_at + skip, REACH), from_east)

    for buf in (halo_depth, halo_guess):
        for at in (0, PAD + ext):
            buf[at : at + PAD, :] = jnp.zeros((PAD, LANES), jnp.float32)
    for at in (0, PAD + ext):
        for buf in (half, half_w, even_e, even_w, odd_e, odd_w):
            buf[:, at : at + PAD, :] = jnp.zeros((tiles + 1, PAD, LANES), jnp.float32)
    near = (lane < EDGE) | (lane >= LANES - EDGE)
    close = (lane < DEEP) | (lane >= LANES - DEEP)
    for at in range(0, ext, LANES):
        block = jnp.transpose(turned[:, at : at + LANES])
        for e in range(at, min(at + LANES, ext), STEP):
            r = e + PAD
            tile = block[e - at : e - at + STEP, :]
            halo_depth[r : r + STEP, :] = jnp.where(near, turn(tile, -40), 0.0)
            halo_guess[r : r + STEP, :] = jnp.where(near, turn(tile, -60), 0.0)
            halo_part[e : e + STEP, :] = jnp.where(close, tile, 0.0)
            fix[e : e + STEP, :] = turn(tile, -80)

    def span(i, by=0):
        return pl.ds(PAD + i * STEP + by, STEP)

    def strip(i):
        return pl.ds(pl.multiple_of(i * STEP, STEP), STEP)

    def read(main, halo, rows):
        return [main[t, rows, :] for t in range(tiles)] + [halo[rows, :]]

    shifted = ((even_e, even_w), (odd_e, odd_w))
    bases = (base0, base1, base2, base3, base4)
    both = range(tiles + 1)
    inner = height // STEP
    above = ROWS // STEP

    def put_beside(values, slot, i):
        east, west = neighbours(values, lane)
        for t in both:
            shifted[slot][0][t, span(i), :] = east[t]
            shifted[slot][1][t, span(i), :] = west[t]

    def prepare(i, c):
        low = [
            jnp.minimum(a, b)
            for a, b in zip(
                read(depth, halo_depth, span(i)), read(depth, halo_depth, span(i, 1))
            )
        ]
        east, _ = neighbours(low, lane)
        corner = [0.5 * jnp.minimum(a, b) for a, b in zip(low, east)]
        _, west = neighbours(corner, lane)
        for t in both:
            half[t, span(i), :] = corner[t]
            half_w[t, span(i), :] = west[t]
        put_beside(read(guess, halo_guess, span(i)), 0, i)
        return c

    sweep(prepare, ext // STEP, WIDE)

    def around(slot, t, i):
        vec_e, vec_w = shifted[slot]
        return (
            (half[t, span(i), :], vec_e[t, span(i, 1), :]),
            (half_w[t, span(i), :], vec_w[t, span(i, 1), :]),
            (half[t, span(i, -1), :], vec_e[t, span(i, -1), :]),
            (half_w[t, span(i, -1), :], vec_w[t, span(i, -1), :]),
        )

    def begin(inside):
        def body(i, c):
            here = read(guess, halo_guess, span(i))
            wide = read(depth, halo_depth, span(i))
            fixes = fix[strip(i), :]
            values = []
            for t in both:
                (ch, ne), (chw, nw), (ch_s, se), (chw_s, sw) = around(0, t, i)
                diagonal = IMPLICIT + ((ch + chw) + (ch_s + chw_s))
                inv = 1.0 / diagonal
                inverse[t, strip(i), :] = inv
                image = IMPLICIT * here[t] + (
                    (ch * (here[t] - ne) + chw * (here[t] - nw))
                    + (ch_s * (here[t] - se) + chw_s * (here[t] - sw))
                )
                total = halo_part[strip(i), :] if t == tiles else part[t, strip(i), :]
                if t == 0:
                    total += jnp.where(lane < REACH, fixes, 0.0)
                if t == tiles - 1:
                    total += jnp.where(lane >= LANES - REACH, fixes, 0.0)
                side = jnp.where(wide[t] > 0.0, total + IMPLICIT * here[t], 0.0)
                values.append((side - image) * inv)
                if inside and t < tiles:
                    base0[t, strip(i - above), :] = values[t]
                    diag[t, strip(i - above), :] = diagonal
            put_beside(values, 1, i)
            return c

        return body

    sweep(begin(True), inner, WIDE_INNER, 0, above)
    sweep(begin(False), 2, 2, 0, 0, above + inner)

    zero = jnp.zeros((STEP, LANES), jnp.float32)

    sums = []
    for j in range(ITERS):
        final = j + 1 == ITERS

        def apply(inside, j=j, final=final):
            def body(i, carry):
                even, odd = carry
                values = []
                for t in both:
                    if final and t == tiles:
                        continue
                    (ch, ne), (chw, nw), (ch_s, se), (chw_s, sw) = around((j + 1) % 2, t, i)
                    value = inverse[t, strip(i), :] * (
                        (ch * ne + chw * nw) + (ch_s * se + chw_s * sw)
                    )
                    values.append(value)
                    if inside and t < tiles:
                        now = bases[j][t, strip(i - above), :]
                        scaled = diag[t, strip(i - above), :] * now
                        even = even + scaled * now
                        odd = odd + scaled * value
                        bases[j + 1][t, strip(i - above), :] = value
                if not final:
                    put_beside(values, j % 2, i)
                return even, odd

            return body

        sums += sweep(apply(True), inner, WIDE_INNER, (zero, zero), above)
        if not final:
            sweep(apply(False), 2, 2, (zero, zero), 0, above + inner)
    lane_row = lax.broadcasted_iota(jnp.int32, (1, LANES), 1)
    found = jnp.zeros((1, LANES), jnp.float32)
    for m in range(2 * ITERS):
        found = jnp.where(lane_row == m, jnp.sum(sums[m]), found)
    for d in range(moments.shape[0]):
        moments[d] = found


def combine_kernel(moments, guess, base0, base1, base2, base3, base4, diag, pressure, residual):
    height, width = pressure.shape
    total = jnp.sum(moments[...], axis=0)
    h = [jnp.broadcast_to(total[:, m : m + 1], (STEP, LANES)) for m in range(2 * ITERS)]
    one, zero = jnp.ones((STEP, LANES), jnp.float32), None

    def plus(a, b):
        return b if a is None else a if b is None else a + b

    def times(a, b):
        return None if a is None or b is None else a * b

    def minus_n(poly):
        moved = [zero] + list(poly)
        return [
            a if b is None else (-b if a is None else a - b)
            for a, b in zip(list(poly) + [zero], moved)
        ]

    def inner(left, right):
        total = None
        for i, a in enumerate(left):
            part = None
            for j, b in enumerate(right):
                part = plus(part, times(b, h[i + j]))
            total = plus(total, times(a, part))
        return total

    rest, direction, answer = [one], [one], []
    norm = h[0]
    for iteration in range(ITERS):
        image = minus_n(direction)
        alpha = norm / inner(direction, image)
        answer = [
            plus(answer[i] if i < len(answer) else None, alpha * c)
            for i, c in enumerate(direction)
        ]
        rest = [
            plus(rest[i] if i < len(rest) else None, -(alpha * c)) for i, c in enumerate(image)
        ]
        if iteration + 1 < ITERS:
            following = inner(rest, rest)
            ratio = following / norm
            direction = [
                plus(c, ratio * direction[i] if i < len(direction) else None)
                for i, c in enumerate(rest)
            ]
            norm = following
    bases = (base0, base1, base2, base3, base4)
    for t in range(width // LANES):
        for o in range(0, height, STEP):
            vecs = [b[t, o : o + STEP, :] for b in bases]
            moved = sum(c * v for c, v in zip(answer, vecs))
            left = sum(c * v for c, v in zip(rest, vecs))
            at = PAD + ROWS + o
            cols = pl.ds(t * LANES, LANES)
            pressure[o : o + STEP, cols] = guess[t, at : at + STEP, :] + moved
            residual[o : o + STEP, cols] = diag[t, o : o + STEP, :] * left


def shift(value, axis, by):
    size = lax.axis_size(axis)
    return lax.ppermute(value, axis, [(i, (i + by) % size) for i in range(size)])


def shards(fields, level_count, thickness, old_pressure):
    levels, height, width = fields.shape[1:]
    ext, tall = height + 2 * ROWS, height + LANES
    f32 = jnp.float32

    def edge(at):
        pick = lambda a: lax.slice_in_dim(a, at, at + ROWS, axis=a.ndim - 2)
        flat = pick(fields).reshape(3 * levels, ROWS, width)
        return jnp.concatenate(
            [flat, pick(level_count).astype(f32)[None], pick(old_pressure)[None]], axis=0
        )

    south = shift(edge(height - ROWS), "by", 1)
    north = shift(edge(0), "by", -1)

    message = message_rows(levels)[3]
    tiles, padded = width // LANES, ext + 2 * PAD
    smem = pl.BlockSpec(memory_space=pltpu.SMEM)
    vmem = pl.BlockSpec(memory_space=pltpu.VMEM)
    whole = lambda *dims: pl.BlockSpec(dims, lambda k: (0,) * len(dims))
    hbm = pl.BlockSpec(memory_space=pltpu.HBM)
    shaped = lambda *dims: jax.ShapeDtypeStruct(dims, f32)
    scratch = lambda *dims: pltpu.VMEM(dims, f32)
    main = (tiles, ext, LANES)
    loose = (tiles, padded, LANES)
    params = lambda size: pltpu.CompilerParams(vmem_limit_bytes=size)
    partial, packed = pl.pallas_call(
        inner_kernel,
        grid=(levels,),
        in_specs=[smem, hbm, hbm],
        out_specs=[whole(*main), whole(ext, LANES)],
        out_shape=[shaped(*main), shaped(ext, LANES)],
        scratch_shapes=[
            scratch(levels, 3, tiles, height + 2 * PAD, LANES),
            scratch(tiles + 1, height + 2 * PAD, LANES),
            pltpu.VMEM((tiles, height, LANES), level_count.dtype),
            pltpu.SemaphoreType.DMA((levels, tiles)),
            pltpu.SemaphoreType.DMA((tiles,)),
        ],
        compiler_params=params(INNER_GRANT),
        cost_estimate=pl.CostEstimate(
            flops=40 * fields.size // 3, bytes_accessed=4 * fields.size, transcendentals=0
        ),
        name="inner_forcing",
    )(thickness, fields, level_count)

    results = (main, loose, loose, (message, tall), (message, tall))
    part, depth, guess, to_east, to_west = pl.pallas_call(
        edge_kernel,
        in_specs=[smem, hbm, vmem, vmem, hbm, hbm, vmem, vmem],
        out_specs=[vmem] * 5,
        out_shape=[shaped(*dims) for dims in results],
        scratch_shapes=[
            scratch(tall, LANES),
            scratch(2, 3, levels, tiles, 3 * ROWS, LANES),
            scratch(2, levels, tiles + 1, 3 * ROWS, LANES),
            scratch(*main),
            scratch(tall, LANES),
            pltpu.VMEM((height, width), level_count.dtype),
            scratch(height, width),
            pltpu.SemaphoreType.DMA((12 * tiles,)),
            pltpu.SemaphoreType.DMA((2,)),
        ],
        compiler_params=params(GRANT),
        name="edge_forcing",
    )(thickness, fields, south, north, level_count, old_pressure, partial, packed)

    from_west = shift(to_east, "bx", 1)
    from_east = shift(to_west, "bx", -1)

    devices = lax.axis_size("by") * lax.axis_size("bx")
    *bases, diag, moments = pl.pallas_call(
        solve_kernel,
        in_specs=[smem] + [vmem] * 7,
        out_specs=[vmem] * (ITERS + 3),
        out_shape=[
            *[shaped(tiles, height, LANES)] * (ITERS + 2),
            shaped(devices, 1, LANES),
        ],
        scratch_shapes=[scratch(LANES, tall), scratch(ext, LANES), scratch(ext, LANES)]
        + [scratch(padded, LANES)] * 2
        + [scratch(tiles + 1, padded, LANES)] * 2
        + [scratch(tiles + 1, ext, LANES)]
        + [scratch(tiles + 1, padded, LANES)] * 4,
        compiler_params=pltpu.CompilerParams(vmem_limit_bytes=GRANT),
        name="krylov",
    )(thickness, part, depth, guess, to_east, to_west, from_west, from_east)

    moments = lax.all_to_all(moments, ("by", "bx"), split_axis=0, concat_axis=0, tiled=True)
    return tuple(
        pl.pallas_call(
            combine_kernel,
            in_specs=[vmem] * (ITERS + 4),
            out_specs=[vmem] * 2,
            out_shape=[shaped(height, width)] * 2,
            compiler_params=pltpu.CompilerParams(vmem_limit_bytes=GRANT),
            name="combine",
        )(moments, guess, *bases, diag)
    )


def solution(mesh):
    placed = (P(None, None, "by", "bx"), P("by", "bx"), P(), P("by", "bx"))
    return jax.shard_map(
        shards,
        mesh=mesh,
        in_specs=placed,
        out_specs=(P("by", "bx"), P("by", "bx")),
        check_vma=False,
    )
```

```python
import math

import jax
import jax.numpy as jnp
from jax import lax
from jax.experimental import pallas as pl
from jax.experimental.pallas import tpu as pltpu
from jax.sharding import PartitionSpec as P

ITERS = 4
VISCOSITY = 0.05
IMPLICIT = 0.05

ROWS = 8
PAD = 8
LANES = 128
REACH = 3
DEEP = ITERS
EDGE = ITERS + 1

STEP = 8
GRANT = 16 * 2**20
INNER_GRANT = 52 * 2**20
CHUNK = 32
WIDE = 17
WIDE_INNER = 16


def message_rows(levels):
    forcing_at = REACH * levels
    count_at = forcing_at + DEEP
    pressure_at = count_at + EDGE
    total = pressure_at + EDGE
    return forcing_at, count_at, pressure_at, -(-total // 8) * 8


def lane_index():
    return lax.broadcasted_iota(jnp.int32, (STEP, LANES), 1)


def turn(value, by):
    return pltpu.roll(value, by % LANES, 1)


def neighbours(tiles, lane, by=1, want_east=True, want_west=True):
    count = len(tiles)
    zero = jnp.zeros((STEP, LANES), jnp.float32)
    east = west = None
    if want_east:
        back = [zero if t is None else turn(t, -by) for t in tiles]
        east = [jnp.where(lane >= LANES - by, back[(i + 1) % count], back[i]) for i in range(count)]
    if want_west:
        forth = [zero if t is None else turn(t, by) for t in tiles]
        west = [jnp.where(lane < by, forth[i - 1], forth[i]) for i in range(count)]
    return east, west


def mix_strip(zonal, merid, mixed, row, lane):
    tiles = zonal.shape[0]
    near = lambda by=0: pl.ds(row + by, STEP)
    east, west = neighbours([zonal[t, near(), :] for t in range(tiles)] + [None], lane)
    for t in range(tiles + 1):
        value = east[t] - west[t]
        if t < tiles:
            value += merid[t, near(1), :] - merid[t, near(-1), :]
        mixed[t, near(), :] = value


def spread_strip(baro, mixed, row, out, at, lane):
    tiles = baro.shape[0]
    both = range(tiles + 1)
    near = lambda by=0: pl.ds(row + by, STEP)
    far, once = [], []
    for t in both:
        own = mixed[t, near(), :]
        beside = mixed[t, near(1), :] + mixed[t, near(-1), :]
        beyond = mixed[t, near(2), :] + mixed[t, near(-2), :]
        once.append(2.0 * beside - 8.0 * own)
        still = beyond - 8.0 * beside + 20.0 * own
        if t < tiles:
            pressure = 10.0 * baro[t, near(), :]
            around = baro[t, near(2), :] + baro[t, near(-2), :]
            own = own + pressure
            still += 10.0 * around - 4.0 * pressure
        far.append(own)
        out[2, t, at, :] = still
    east, west = neighbours(far, lane)
    for t in both:
        out[0, t, at, :] = once[t] + east[t]
        out[1, t, at, :] = once[t] + west[t]


def gather_strip(staged, at, lane):
    both = range(staged.shape[1])
    east, _ = neighbours([staged[0, t, at, :] for t in both], lane, 1, True, False)
    _, west = neighbours([staged[1, t, at, :] for t in both], lane, 1, False, True)
    return [staged[2, t, at, :] + (east[t] + west[t]) for t in both]


def sweep(body, strips, unroll, carry=0, first=0, stride=1):
    step = lambda i, c: body(first + stride * i, c)
    return lax.fori_loop(0, strips, step, carry, unroll=unroll)


def lane_tiles(tiles):
    return [pl.ds(t * LANES, LANES) for t in range(tiles)]


def inner_kernel(
    thick, fields, count_hbm, part, pack, block, mixed, staged, beyond, count, arrivals, others
):
    levels = fields.shape[1]
    tiles, height, _ = count.shape
    lane = lane_index()
    cols = lane_tiles(tiles)
    strips = height // STEP
    size = math.gcd(strips, CHUNK)

    def arrival(at, t):
        return pltpu.make_async_copy(
            fields.at[:, at, :, cols[t]], block.at[at, :, t, pl.ds(PAD, height), :], arrivals.at[at, t]
        )

    counted = [
        pltpu.make_async_copy(count_hbm.at[:, cols[t]], count.at[t], others.at[t])
        for t in range(tiles)
    ]
    for at in range(levels):
        for t in range(tiles):
            arrival(at, t).start()
    for copy in counted:
        copy.start()
    part[...] = jnp.zeros_like(part)
    pack[...] = jnp.zeros_like(pack)

    def mix(n, c):
        chunks = strips // size
        level, chunk = lax.div(n, chunks), lax.rem(n, chunks)

        @pl.when(chunk == 0)
        def _():
            for t in range(tiles):
                arrival(level, t).wait()

        for q in range(size):
            row = PAD + pl.multiple_of(chunk * (size * STEP), STEP) + q * STEP
            mix_strip(block.at[level, 0], block.at[level, 1], mixed.at[level], row, lane)
        return c

    def chunked(body):
        chunks = strips // size

        def step(n, c):
            level, chunk = lax.div(n, chunks), lax.rem(n, chunks)
            for q in range(size):
                body(level, pl.multiple_of(chunk * (size * STEP), STEP) + q * STEP)
            return c

        sweep(step, levels * chunks, 1)

    def spread(level, row):
        at = pl.ds(row, STEP)
        spread_strip(block.at[level, 2], mixed.at[level], PAD + row, staged.at[level], at, lane)

    def weigh(level, row):
        at, rows = pl.ds(row, STEP), pl.ds(ROWS + row, STEP)
        total = gather_strip(staged.at[level], at, lane)
        for t in range(tiles):
            weight = jnp.where(count[t, at, :] > level, thick[level], 0.0)
            part[t, rows, :] += weight * total[t]
        beyond[level, at, :] = total[tiles]

    def put(level, row):
        rows = pl.ds(ROWS + row, STEP)
        pack[rows, :] += pltpu.roll(beyond[level, pl.ds(row, STEP), :], 8 * level + REACH, 1)

    sweep(mix, levels * (strips // size), 1)
    for copy in counted:
        copy.wait()
    chunked(spread)
    chunked(weigh)
    chunked(put)


def edge_kernel(
    thick, fields, south, north, count_hbm, old_hbm, part_in, pack_in,
    part, depth, guess, to_east, to_west,
    pack, block, mixed, staged, beyond, wet, edges, count, old, arrivals, others,
):
    levels = fields.shape[1]
    height, width = count.shape
    tiles = width // LANES
    ext = height + 2 * ROWS
    forcing_at = message_rows(levels)[0]
    lane = lane_index()
    cols = lane_tiles(tiles)

    copies = [
        pltpu.make_async_copy(count_hbm, count, others.at[0]),
        pltpu.make_async_copy(old_hbm, old, others.at[1]),
    ]
    for f in range(3):
        for t, c in enumerate(cols):
            for side, (here, there, halo, row) in enumerate(
                ((ROWS, 0, south, 0), (0, 2 * ROWS, north, height - 2 * ROWS))
            ):
                at = 4 * (f * tiles + t) + 2 * side
                group = block.at[side, f, :, t]
                copies += [
                    pltpu.make_async_copy(
                        fields.at[f, :, pl.ds(row, 2 * ROWS), c],
                        group.at[:, pl.ds(here, 2 * ROWS), :],
                        arrivals.at[at],
                    ),
                    pltpu.make_async_copy(
                        halo.at[pl.ds(f * levels, levels), :, c],
                        group.at[:, pl.ds(there, ROWS), :],
                        arrivals.at[at + 1],
                    ),
                ]
    for copy in copies:
        copy.start()
    low, high = slice(0, ROWS - DEEP), slice(ext - (ROWS - DEEP), ext)
    for buf in (depth, guess):
        for at in (0, PAD + ext):
            buf[:, at : at + PAD, :] = jnp.zeros((tiles, PAD, LANES), jnp.float32)
    inner = slice(2 * ROWS - DEEP, ext - (2 * ROWS - DEEP))
    part[:, inner, :] = part_in[:, inner, :]
    pack[inner, :] = pack_in[inner, :]
    for outer in (low, high, slice(ext, pack.shape[0])):
        if outer.start < ext:
            part[:, outer, :] = jnp.zeros((tiles, ROWS - DEEP, LANES), jnp.float32)
        pack[outer, :] = jnp.zeros((outer.stop - outer.start, LANES), jnp.float32)
    edges[ext:, :] = jnp.zeros((edges.shape[0] - ext, LANES), jnp.float32)
    for copy in copies:
        copy.wait()
    for t, c in enumerate(cols):
        wet[t, :ROWS, :] = south[3 * levels, :, c]
        wet[t, ROWS : ROWS + height, :] = count[:, c].astype(jnp.float32)
        wet[t, ROWS + height :, :] = north[3 * levels, :, c]

    plans = ((ROWS - DEEP, (2, 10)), (2 * ROWS - DEEP, (10, 14)))
    starts = (ROWS - DEEP, ext - (2 * ROWS - DEEP))

    def mix(k, c):
        for side, (_, rows) in enumerate(plans):
            for row in rows:
                mix_strip(block.at[side, 0, k], block.at[side, 1, k], mixed.at[side, k], row, lane)
        return c

    every = pl.ds(0, STEP)

    def spread(k, c):
        for side, (row, _) in enumerate(plans):
            spread_strip(block.at[side, 2, k], mixed.at[side, k], row, staged.at[side, k], every, lane)
        return c

    def weigh(k, carry):
        found = []
        number, thickness = k.astype(jnp.float32), thick[k]
        for side, e in enumerate(starts):
            total = gather_strip(staged.at[side, k], every, lane)
            for t in range(tiles):
                weight = jnp.where(wet[t, e : e + STEP, :] > number, thickness, 0.0)
                found.append(weight * total[t])
            beyond[side, k] = total[tiles]
        return tuple(a + b for a, b in zip(carry, found))

    sweep(mix, levels, 4)
    sweep(spread, levels, 4)
    zero = jnp.zeros((STEP, LANES), jnp.float32)
    found = sweep(weigh, levels, 4, (zero,) * (2 * tiles))
    for side, e in enumerate(starts):
        for t in range(tiles):
            part[t, e : e + STEP, :] = found[side * tiles + t]
        pack[e : e + STEP, :] = sum(turn(beyond[side, k], 8 * k + REACH) for k in range(levels))

    scale = -0.5 * VISCOSITY
    for e in range(0, ext, STEP):
        r = e + PAD
        begin = []
        for t, c in enumerate(cols):
            if e < ROWS:
                pressure = south[3 * levels + 1, :, c]
            elif e >= ROWS + height:
                pressure = north[3 * levels + 1, :, c]
            else:
                pressure = old[e - ROWS : e - ROWS + STEP, c]
            counts = wet[t, e : e + STEP, :]
            depth[t, r : r + STEP, :] = sum(
                jnp.where(counts > float(k), thick[k], 0.0) for k in range(levels)
            )
            begin.append(jnp.where(counts > 0.0, pressure, 0.0))
            guess[t, r : r + STEP, :] = begin[t]
            part[t, e : e + STEP, :] *= scale
        tile = None
        for t, inside, start in ((tiles - 1, True, 0), (0, False, LANES // 2)):
            at = start
            for piece, size in (
                (part[t, e : e + STEP, :], DEEP),
                (wet[t, e : e + STEP, :], EDGE),
                (begin[t], EDGE),
            ):
                moved = turn(piece, at + size if inside else at)
                mask = (lane >= at) & (lane < at + size)
                tile = jnp.where(mask, moved, 0.0 if tile is None else tile)
                at += size
        edges[e : e + STEP, :] = tile
    size = DEEP + 2 * EDGE
    for message in (to_east, to_west):
        message[...] = jnp.zeros_like(message)
    for at in range(0, to_east.shape[1], LANES):
        span = slice(at, at + LANES)
        turned = scale * jnp.transpose(pack[span, :])
        for k in range(levels):
            mine = slice(REACH * k, REACH * k + REACH)
            to_west[mine, span] = turned[8 * k : 8 * k + REACH, :]
            to_east[mine, span] = turned[8 * k + REACH : 8 * k + 2 * REACH, :]
        turned = jnp.transpose(edges[span, :])
        to_east[forcing_at : forcing_at + size, span] = turned[:size, :]
        to_west[forcing_at : forcing_at + size, span] = turned[LANES // 2 : LANES // 2 + size, :]


def solve_kernel(
    thick, part, depth, guess, to_east, to_west, from_west, from_east,
    base0, base1, base2, base3, base4, diag, moments,
    turned, upright, fix, halo_part, halo_depth, halo_guess, half, half_w, inverse, even_e, even_w, odd_e, odd_w,
):
    tiles, ext, _ = part.shape
    height = ext - 2 * ROWS
    levels = thick.shape[0]
    forcing_at, count_at, pressure_at, _ = message_rows(levels)
    lane = lane_index()

    def weights(counts):
        return [jnp.where(counts > float(k), thick[k], 0.0) for k in range(levels)]

    def weighted(counts, message):
        total = None
        for k, weight in enumerate(weights(counts)):
            term = weight * message[REACH * k : REACH * k + REACH, :]
            total = term if total is None else total + term
        return total

    def rows(message, at, size):
        return message[at : at + size, :]

    skip = EDGE - REACH
    turned[...] = jnp.zeros_like(turned)
    turned[0:DEEP, :] = rows(from_east, forcing_at, DEEP)
    turned[0:REACH, :] += weighted(rows(from_east, count_at, REACH), to_east)
    turned[LANES - DEEP : LANES, :] = rows(from_west, forcing_at, DEEP)
    turned[LANES - REACH : LANES, :] += weighted(rows(from_west, count_at + skip, REACH), to_west)
    turned[40 : 40 + EDGE, :] = sum(weights(rows(from_east, count_at, EDGE)))
    turned[40 - EDGE : 40, :] = sum(weights(rows(from_west, count_at, EDGE)))
    turned[60 : 60 + EDGE, :] = rows(from_east, pressure_at, EDGE)
    turned[60 - EDGE : 60, :] = rows(from_west, pressure_at, EDGE)
    turned[80 : 80 + REACH, :] = weighted(rows(to_west, count_at, REACH), from_west)
    turned[80 - REACH : 80, :] = weighted(rows(to_east, count_at + skip, REACH), from_east)

    for buf in (halo_depth, halo_guess):
        for at in (0, PAD + ext):
            buf[at : at + PAD, :] = jnp.zeros((PAD, LANES), jnp.float32)
    for at in (0, PAD + ext):
        for buf in (half, half_w, even_e, even_w, odd_e, odd_w):
            buf[:, at : at + PAD, :] = jnp.zeros((tiles + 1, PAD, LANES), jnp.float32)
    near = (lane < EDGE) | (lane >= LANES - EDGE)
    close = (lane < DEEP) | (lane >= LANES - DEEP)
    for at in range(0, turned.shape[1], LANES):
        upright[at : at + LANES, :] = jnp.transpose(turned[:, at : at + LANES])
    for e in range(0, ext, STEP):
        r = e + PAD
        tile = upright[e : e + STEP, :]
        halo_depth[r : r + STEP, :] = jnp.where(near, turn(tile, -40), 0.0)
        halo_guess[r : r + STEP, :] = jnp.where(near, turn(tile, -60), 0.0)
        halo_part[e : e + STEP, :] = jnp.where(close, tile, 0.0)
        fix[e : e + STEP, :] = turn(tile, -80)

    def span(i, by=0):
        return pl.ds(PAD + i * STEP + by, STEP)

    def strip(i):
        return pl.ds(pl.multiple_of(i * STEP, STEP), STEP)

    def read(main, halo, rows):
        return [main[t, rows, :] for t in range(tiles)] + [halo[rows, :]]

    shifted = ((even_e, even_w), (odd_e, odd_w))
    bases = (base0, base1, base2, base3, base4)
    both = range(tiles + 1)
    inner = height // STEP
    above = ROWS // STEP

    def put_beside(values, slot, i):
        east, west = neighbours(values, lane)
        for t in both:
            shifted[slot][0][t, span(i), :] = east[t]
            shifted[slot][1][t, span(i), :] = west[t]

    def prepare(i, c):
        low = [
            jnp.minimum(a, b)
            for a, b in zip(
                read(depth, halo_depth, span(i)), read(depth, halo_depth, span(i, 1))
            )
        ]
        east, west = neighbours(low, lane)
        corner = [0.5 * jnp.minimum(a, b) for a, b in zip(low, east)]
        west = [0.5 * jnp.minimum(a, b) for a, b in zip(low, west)]
        for t in both:
            half[t, span(i), :] = corner[t]
            half_w[t, span(i), :] = west[t]
        put_beside(read(guess, halo_guess, span(i)), 0, i)
        return c

    sweep(prepare, ext // STEP, WIDE)

    def around(slot, t, i):
        vec_e, vec_w = shifted[slot]
        return (
            (half[t, span(i), :], vec_e[t, span(i, 1), :]),
            (half_w[t, span(i), :], vec_w[t, span(i, 1), :]),
            (half[t, span(i, -1), :], vec_e[t, span(i, -1), :]),
            (half_w[t, span(i, -1), :], vec_w[t, span(i, -1), :]),
        )

    def begin(inside):
        def body(i, c):
            here = read(guess, halo_guess, span(i))
            wide = read(depth, halo_depth, span(i))
            fixes = fix[strip(i), :]
            values = []
            for t in both:
                (ch, ne), (chw, nw), (ch_s, se), (chw_s, sw) = around(0, t, i)
                diagonal = IMPLICIT + ((ch + chw) + (ch_s + chw_s))
                inv = 1.0 / diagonal
                inverse[t, strip(i), :] = inv
                image = IMPLICIT * here[t] + (
                    (ch * (here[t] - ne) + chw * (here[t] - nw))
                    + (ch_s * (here[t] - se) + chw_s * (here[t] - sw))
                )
                total = halo_part[strip(i), :] if t == tiles else part[t, strip(i), :]
                if t == 0:
                    total += jnp.where(lane < REACH, fixes, 0.0)
                if t == tiles - 1:
                    total += jnp.where(lane >= LANES - REACH, fixes, 0.0)
                side = jnp.where(wide[t] > 0.0, total + IMPLICIT * here[t], 0.0)
                values.append((side - image) * inv)
                if inside and t < tiles:
                    base0[t, strip(i - above), :] = values[t]
                    diag[t, strip(i - above), :] = diagonal
            put_beside(values, 1, i)
            return c

        return body

    sweep(begin(True), inner, WIDE_INNER, 0, above)
    sweep(begin(False), 2, 2, 0, 0, above + inner)

    zero = jnp.zeros((STEP, LANES), jnp.float32)

    sums = []
    for j in range(ITERS):
        final = j + 1 == ITERS

        def apply(inside, j=j, final=final):
            def body(i, carry):
                even, odd = carry
                values = []
                for t in both:
                    if final and t == tiles:
                        continue
                    (ch, ne), (chw, nw), (ch_s, se), (chw_s, sw) = around((j + 1) % 2, t, i)
                    value = inverse[t, strip(i), :] * (
                        (ch * ne + chw * nw) + (ch_s * se + chw_s * sw)
                    )
                    values.append(value)
                    if inside and t < tiles:
                        now = bases[j][t, strip(i - above), :]
                        scaled = diag[t, strip(i - above), :] * now
                        even = even + scaled * now
                        odd = odd + scaled * value
                        bases[j + 1][t, strip(i - above), :] = value
                if not final:
                    put_beside(values, j % 2, i)
                return even, odd

            return body

        sums += sweep(apply(True), inner, WIDE_INNER, (zero, zero), above)
        if not final:
            sweep(apply(False), 2, 2, (zero, zero), 0, above + inner)
    lane_row = lax.broadcasted_iota(jnp.int32, (1, LANES), 1)
    found = jnp.zeros((1, LANES), jnp.float32)
    for m in range(2 * ITERS):
        found = jnp.where(lane_row == m, jnp.sum(sums[m]), found)
    for d in range(moments.shape[0]):
        moments[d] = found


def combine_kernel(moments, guess, base0, base1, base2, base3, base4, diag, pressure, residual):
    height, width = pressure.shape
    total = jnp.sum(moments[...], axis=0)
    h = [jnp.broadcast_to(total[:, m : m + 1], (STEP, LANES)) for m in range(2 * ITERS)]
    one, zero = jnp.ones((STEP, LANES), jnp.float32), None

    def plus(a, b):
        return b if a is None else a if b is None else a + b

    def times(a, b):
        return None if a is None or b is None else a * b

    def minus_n(poly):
        moved = [zero] + list(poly)
        return [
            a if b is None else (-b if a is None else a - b)
            for a, b in zip(list(poly) + [zero], moved)
        ]

    def inner(left, right):
        total = None
        for i, a in enumerate(left):
            part = None
            for j, b in enumerate(right):
                part = plus(part, times(b, h[i + j]))
            total = plus(total, times(a, part))
        return total

    rest, direction, answer = [one], [one], []
    norm = h[0]
    for iteration in range(ITERS):
        image = minus_n(direction)
        alpha = norm / inner(direction, image)
        answer = [
            plus(answer[i] if i < len(answer) else None, alpha * c)
            for i, c in enumerate(direction)
        ]
        rest = [
            plus(rest[i] if i < len(rest) else None, -(alpha * c)) for i, c in enumerate(image)
        ]
        if iteration + 1 < ITERS:
            following = inner(rest, rest)
            ratio = following / norm
            direction = [
                plus(c, ratio * direction[i] if i < len(direction) else None)
                for i, c in enumerate(rest)
            ]
            norm = following
    bases = (base0, base1, base2, base3, base4)
    for t in range(width // LANES):
        for o in range(0, height, STEP):
            vecs = [b[t, o : o + STEP, :] for b in bases]
            moved = sum(c * v for c, v in zip(answer, vecs))
            left = sum(c * v for c, v in zip(rest, vecs))
            at = PAD + ROWS + o
            cols = pl.ds(t * LANES, LANES)
            pressure[o : o + STEP, cols] = guess[t, at : at + STEP, :] + moved
            residual[o : o + STEP, cols] = diag[t, o : o + STEP, :] * left


def shift(value, axis, by):
    size = lax.axis_size(axis)
    return lax.ppermute(value, axis, [(i, (i + by) % size) for i in range(size)])


def shards(fields, level_count, thickness, old_pressure):
    levels, height, width = fields.shape[1:]
    ext, tall = height + 2 * ROWS, height + LANES
    f32 = jnp.float32

    def edge(at):
        pick = lambda a: lax.slice_in_dim(a, at, at + ROWS, axis=a.ndim - 2)
        flat = pick(fields).reshape(3 * levels, ROWS, width)
        return jnp.concatenate(
            [flat, pick(level_count).astype(f32)[None], pick(old_pressure)[None]], axis=0
        )

    south = shift(edge(height - ROWS), "by", 1)
    north = shift(edge(0), "by", -1)

    message = message_rows(levels)[3]
    tiles, padded = width // LANES, ext + 2 * PAD
    smem = pl.BlockSpec(memory_space=pltpu.SMEM)
    vmem = pl.BlockSpec(memory_space=pltpu.VMEM)
    hbm = pl.BlockSpec(memory_space=pltpu.HBM)
    shaped = lambda *dims: jax.ShapeDtypeStruct(dims, f32)
    scratch = lambda *dims: pltpu.VMEM(dims, f32)
    main = (tiles, ext, LANES)
    loose = (tiles, padded, LANES)
    params = lambda size: pltpu.CompilerParams(vmem_limit_bytes=size)
    partial, packed = pl.pallas_call(
        inner_kernel,
        in_specs=[smem, hbm, hbm],
        out_specs=[vmem] * 2,
        out_shape=[shaped(*main), shaped(ext, LANES)],
        scratch_shapes=[
            scratch(levels, 3, tiles, height + 2 * PAD, LANES),
            scratch(levels, tiles + 1, height + 2 * PAD, LANES),
            scratch(levels, 3, tiles + 1, height, LANES),
            scratch(levels, height, LANES),
            pltpu.VMEM((tiles, height, LANES), level_count.dtype),
            pltpu.SemaphoreType.DMA((levels, tiles)),
            pltpu.SemaphoreType.DMA((tiles,)),
        ],
        compiler_params=params(INNER_GRANT),
        cost_estimate=pl.CostEstimate(
            flops=40 * fields.size // 3, bytes_accessed=4 * fields.size, transcendentals=0
        ),
        name="inner_forcing",
    )(thickness, fields, level_count)

    results = (main, loose, loose, (message, tall), (message, tall))
    part, depth, guess, to_east, to_west = pl.pallas_call(
        edge_kernel,
        in_specs=[smem, hbm, vmem, vmem, hbm, hbm, vmem, vmem],
        out_specs=[vmem] * 5,
        out_shape=[shaped(*dims) for dims in results],
        scratch_shapes=[
            scratch(tall, LANES),
            scratch(2, 3, levels, tiles, 3 * ROWS, LANES),
            scratch(2, levels, tiles + 1, 3 * ROWS, LANES),
            scratch(2, levels, 3, tiles + 1, STEP, LANES),
            scratch(2, levels, STEP, LANES),
            scratch(*main),
            scratch(tall, LANES),
            pltpu.VMEM((height, width), level_count.dtype),
            scratch(height, width),
            pltpu.SemaphoreType.DMA((12 * tiles,)),
            pltpu.SemaphoreType.DMA((2,)),
        ],
        compiler_params=params(GRANT),
        name="edge_forcing",
    )(thickness, fields, south, north, level_count, old_pressure, partial, packed)

    from_west = shift(to_east, "bx", 1)
    from_east = shift(to_west, "bx", -1)

    devices = lax.axis_size("by") * lax.axis_size("bx")
    *bases, diag, moments = pl.pallas_call(
        solve_kernel,
        in_specs=[smem] + [vmem] * 7,
        out_specs=[vmem] * (ITERS + 3),
        out_shape=[
            *[shaped(tiles, height, LANES)] * (ITERS + 2),
            shaped(devices, 1, LANES),
        ],
        scratch_shapes=[scratch(LANES, tall), scratch(tall, LANES)]
        + [scratch(ext, LANES)] * 2
        + [scratch(padded, LANES)] * 2
        + [scratch(tiles + 1, padded, LANES)] * 2
        + [scratch(tiles + 1, ext, LANES)]
        + [scratch(tiles + 1, padded, LANES)] * 4,
        compiler_params=pltpu.CompilerParams(vmem_limit_bytes=GRANT),
        name="krylov",
    )(thickness, part, depth, guess, to_east, to_west, from_west, from_east)

    moments = lax.all_to_all(moments, ("by", "bx"), split_axis=0, concat_axis=0, tiled=True)
    return tuple(
        pl.pallas_call(
            combine_kernel,
            in_specs=[vmem] * (ITERS + 4),
            out_specs=[vmem] * 2,
            out_shape=[shaped(height, width)] * 2,
            compiler_params=pltpu.CompilerParams(vmem_limit_bytes=GRANT),
            name="combine",
        )(moments, guess, *bases, diag)
    )


def solution(mesh):
    placed = (P(None, None, "by", "bx"), P("by", "bx"), P(), P("by", "bx"))
    return jax.shard_map(
        shards,
        mesh=mesh,
        in_specs=placed,
        out_specs=(P("by", "bx"), P("by", "bx")),
        check_vma=False,
    )
```

```python
import math

import jax
import jax.numpy as jnp
from jax import lax
from jax.experimental import pallas as pl
from jax.experimental.pallas import tpu as pltpu
from jax.sharding import PartitionSpec as P

ITERS = 4
VISCOSITY = 0.05
IMPLICIT = 0.05

ROWS = 8
PAD = 8
LANES = 128
REACH = 3
DEEP = ITERS
EDGE = ITERS + 1

STEP = 8
GRANT = 16 * 2**20
INNER_GRANT = 52 * 2**20
CHUNK = 32
WIDE = 34
WIDE_INNER = 32


def message_rows(levels):
    forcing_at = REACH * levels
    count_at = forcing_at + DEEP
    pressure_at = count_at + EDGE
    total = pressure_at + EDGE
    return forcing_at, count_at, pressure_at, -(-total // 8) * 8


def lane_index():
    return lax.broadcasted_iota(jnp.int32, (STEP, LANES), 1)


def turn(value, by):
    return pltpu.roll(value, by % LANES, 1)


def neighbours(tiles, lane, by=1, want_east=True, want_west=True):
    count = len(tiles)
    zero = jnp.zeros((STEP, LANES), jnp.float32)
    east = west = None
    if want_east:
        back = [zero if t is None else turn(t, -by) for t in tiles]
        east = [jnp.where(lane >= LANES - by, back[(i + 1) % count], back[i]) for i in range(count)]
    if want_west:
        forth = [zero if t is None else turn(t, by) for t in tiles]
        west = [jnp.where(lane < by, forth[i - 1], forth[i]) for i in range(count)]
    return east, west


def mix_strip(zonal, merid, mixed, row, lane):
    tiles = zonal.shape[0]
    near = lambda by=0: pl.ds(row + by, STEP)
    east, west = neighbours([zonal[t, near(), :] for t in range(tiles)] + [None], lane)
    for t in range(tiles + 1):
        value = east[t] - west[t]
        if t < tiles:
            value += merid[t, near(1), :] - merid[t, near(-1), :]
        mixed[t, near(), :] = value


def spread_strip(baro, mixed, row, out, at, lane):
    tiles = baro.shape[0]
    both = range(tiles + 1)
    near = lambda by=0: pl.ds(row + by, STEP)
    far, once = [], []
    for t in both:
        own = mixed[t, near(), :]
        beside = mixed[t, near(1), :] + mixed[t, near(-1), :]
        beyond = mixed[t, near(2), :] + mixed[t, near(-2), :]
        once.append(2.0 * beside - 8.0 * own)
        still = beyond - 8.0 * beside + 20.0 * own
        if t < tiles:
            pressure = 10.0 * baro[t, near(), :]
            around = baro[t, near(2), :] + baro[t, near(-2), :]
            own = own + pressure
            still += 10.0 * around - 4.0 * pressure
        far.append(own)
        out[2, t, at, :] = still
    east, west = neighbours(far, lane)
    for t in both:
        out[0, t, at, :] = once[t] + east[t]
        out[1, t, at, :] = once[t] + west[t]


def gather_strip(staged, at, lane):
    both = range(staged.shape[1])
    east, _ = neighbours([staged[0, t, at, :] for t in both], lane, 1, True, False)
    _, west = neighbours([staged[1, t, at, :] for t in both], lane, 1, False, True)
    return [staged[2, t, at, :] + (east[t] + west[t]) for t in both]


def sweep(body, strips, unroll, carry=0, first=0, stride=1):
    step = lambda i, c: body(first + stride * i, c)
    return lax.fori_loop(0, strips, step, carry, unroll=unroll)


def lane_tiles(tiles):
    return [pl.ds(t * LANES, LANES) for t in range(tiles)]


def inner_kernel(
    thick, fields, counts, part, beyond, block, mixed, staged, arrivals
):
    levels = fields.shape[1]
    height, width = counts.shape
    tiles = width // LANES
    lane = lane_index()
    cols = lane_tiles(tiles)
    strips = height // STEP
    size = math.gcd(strips, CHUNK)

    def arrival(at, t):
        return pltpu.make_async_copy(
            fields.at[:, at, :, cols[t]], block.at[at, :, t, pl.ds(PAD, height), :], arrivals.at[at, t]
        )

    for at in range(levels):
        for t in range(tiles):
            arrival(at, t).start()
    part[...] = jnp.zeros_like(part)

    def mix(n, c):
        chunks = strips // size
        level, chunk = lax.div(n, chunks), lax.rem(n, chunks)

        @pl.when(chunk == 0)
        def _():
            for t in range(tiles):
                arrival(level, t).wait()

        for q in range(size):
            row = PAD + pl.multiple_of(chunk * (size * STEP), STEP) + q * STEP
            mix_strip(block.at[level, 0], block.at[level, 1], mixed.at[level], row, lane)
        return c

    def chunked(body):
        chunks = strips // size

        def step(n, c):
            level, chunk = lax.div(n, chunks), lax.rem(n, chunks)
            for q in range(size):
                body(level, pl.multiple_of(chunk * (size * STEP), STEP) + q * STEP)
            return c

        sweep(step, levels * chunks, 2)

    def spread(level, row):
        at = pl.ds(row, STEP)
        spread_strip(block.at[level, 2], mixed.at[level], PAD + row, staged.at[level], at, lane)

    def weigh(level, row):
        at, rows = pl.ds(row, STEP), pl.ds(ROWS + row, STEP)
        total = gather_strip(staged.at[level], at, lane)
        number = level.astype(jnp.float32)
        for t in range(tiles):
            weight = jnp.where(counts[at, cols[t]] > number, thick[level], 0.0)
            part[t, rows, :] += weight * total[t]
        beyond[level, at, :] = total[tiles]

    sweep(mix, levels * (strips // size), 1)
    chunked(spread)
    chunked(weigh)


def edge_kernel(
    thick, fields, south, north, counts, old_hbm, part_in, beyond_in,
    part, depth, guess, to_east, to_west,
    block, mixed, staged, beyond, wet, edges, old, arrivals, others,
):
    levels = fields.shape[1]
    height, width = counts.shape
    tiles = width // LANES
    ext = height + 2 * ROWS
    forcing_at = message_rows(levels)[0]
    lane = lane_index()
    cols = lane_tiles(tiles)

    copies = [
        pltpu.make_async_copy(old_hbm, old, others.at[0]),
    ]
    for f in range(3):
        for t, c in enumerate(cols):
            for side, (here, there, halo, row) in enumerate(
                ((ROWS, 0, south, 0), (0, 2 * ROWS, north, height - 2 * ROWS))
            ):
                at = 4 * (f * tiles + t) + 2 * side
                group = block.at[side, f, :, t]
                copies += [
                    pltpu.make_async_copy(
                        fields.at[f, :, pl.ds(row, 2 * ROWS), c],
                        group.at[:, pl.ds(here, 2 * ROWS), :],
                        arrivals.at[at],
                    ),
                    pltpu.make_async_copy(
                        halo.at[pl.ds(f * levels, levels), :, c],
                        group.at[:, pl.ds(there, ROWS), :],
                        arrivals.at[at + 1],
                    ),
                ]
    for copy in copies:
        copy.start()
    low, high = slice(0, ROWS - DEEP), slice(ext - (ROWS - DEEP), ext)
    for buf in (depth, guess):
        for at in (0, PAD + ext):
            buf[:, at : at + PAD, :] = jnp.zeros((tiles, PAD, LANES), jnp.float32)
    inner = slice(2 * ROWS - DEEP, ext - (2 * ROWS - DEEP))
    part[:, inner, :] = part_in[:, inner, :]
    beyond[:, inner, :] = beyond_in[:, inner.start - ROWS : inner.stop - ROWS, :]
    for outer in (low, high):
        part[:, outer, :] = jnp.zeros((tiles, ROWS - DEEP, LANES), jnp.float32)
    for outer in (low, slice(high.start, beyond.shape[1])):
        beyond[:, outer, :] = jnp.zeros((levels, outer.stop - outer.start, LANES), jnp.float32)
    edges[ext:, :] = jnp.zeros((edges.shape[0] - ext, LANES), jnp.float32)
    for copy in copies:
        copy.wait()
    for t, c in enumerate(cols):
        wet[t, :ROWS, :] = south[3 * levels, :, c]
        wet[t, ROWS : ROWS + height, :] = counts[:, c]
        wet[t, ROWS + height :, :] = north[3 * levels, :, c]

    plans = ((ROWS - DEEP, (2, 10)), (2 * ROWS - DEEP, (10, 14)))
    starts = (ROWS - DEEP, ext - (2 * ROWS - DEEP))

    def mix(k, c):
        for side, (_, rows) in enumerate(plans):
            for row in rows:
                mix_strip(block.at[side, 0, k], block.at[side, 1, k], mixed.at[side, k], row, lane)
        return c

    every = pl.ds(0, STEP)

    def spread(k, c):
        for side, (row, _) in enumerate(plans):
            spread_strip(block.at[side, 2, k], mixed.at[side, k], row, staged.at[side, k], every, lane)
        return c

    def weigh(k, carry):
        found = []
        number, thickness = k.astype(jnp.float32), thick[k]
        for side, e in enumerate(starts):
            total = gather_strip(staged.at[side, k], every, lane)
            for t in range(tiles):
                weight = jnp.where(wet[t, e : e + STEP, :] > number, thickness, 0.0)
                found.append(weight * total[t])
            beyond[k, e : e + STEP, :] = total[tiles]
        return tuple(a + b for a, b in zip(carry, found))

    sweep(mix, levels, levels)
    sweep(spread, levels, levels)
    zero = jnp.zeros((STEP, LANES), jnp.float32)
    found = sweep(weigh, levels, levels, (zero,) * (2 * tiles))
    for side, e in enumerate(starts):
        for t in range(tiles):
            part[t, e : e + STEP, :] = found[side * tiles + t]

    scale = -0.5 * VISCOSITY
    for e in range(0, ext, STEP):
        r = e + PAD
        begin = []
        for t, c in enumerate(cols):
            if e < ROWS:
                pressure = south[3 * levels + 1, :, c]
            elif e >= ROWS + height:
                pressure = north[3 * levels + 1, :, c]
            else:
                pressure = old[e - ROWS : e - ROWS + STEP, c]
            counts = wet[t, e : e + STEP, :]
            depth[t, r : r + STEP, :] = sum(
                jnp.where(counts > float(k), thick[k], 0.0) for k in range(levels)
            )
            begin.append(jnp.where(counts > 0.0, pressure, 0.0))
            guess[t, r : r + STEP, :] = begin[t]
            part[t, e : e + STEP, :] *= scale
        tile = None
        for t, inside, start in ((tiles - 1, True, 0), (0, False, LANES // 2)):
            at = start
            for piece, size in (
                (part[t, e : e + STEP, :], DEEP),
                (wet[t, e : e + STEP, :], EDGE),
                (begin[t], EDGE),
            ):
                moved = turn(piece, at + size if inside else at)
                mask = (lane >= at) & (lane < at + size)
                tile = jnp.where(mask, moved, 0.0 if tile is None else tile)
                at += size
        edges[e : e + STEP, :] = tile
    size = DEEP + 2 * EDGE
    for message in (to_east, to_west):
        message[...] = jnp.zeros_like(message)
    for at in range(0, to_east.shape[1], LANES):
        span = slice(at, at + LANES)
        for k in range(levels):
            mine = slice(REACH * k, REACH * k + REACH)
            turned = scale * jnp.transpose(beyond[k, span, :])
            to_west[mine, span] = turned[LANES - REACH :, :]
            to_east[mine, span] = turned[:REACH, :]
        turned = jnp.transpose(edges[span, :])
        to_east[forcing_at : forcing_at + size, span] = turned[:size, :]
        to_west[forcing_at : forcing_at + size, span] = turned[LANES // 2 : LANES // 2 + size, :]


def solve_kernel(
    thick, part, depth, guess, to_east, to_west, from_west, from_east,
    base0, base1, base2, base3, base4, diag, moments,
    turned, upright, fix, halo_part, halo_depth, halo_guess, half, half_w, inverse, even_e, even_w, odd_e, odd_w,
):
    tiles, ext, _ = part.shape
    height = ext - 2 * ROWS
    levels = thick.shape[0]
    forcing_at, count_at, pressure_at, _ = message_rows(levels)
    lane = lane_index()

    def weights(counts):
        return [jnp.where(counts > float(k), thick[k], 0.0) for k in range(levels)]

    def weighted(counts, message):
        total = None
        for k, weight in enumerate(weights(counts)):
            term = weight * message[REACH * k : REACH * k + REACH, :]
            total = term if total is None else total + term
        return total

    def rows(message, at, size):
        return message[at : at + size, :]

    skip = EDGE - REACH
    turned[...] = jnp.zeros_like(turned)
    turned[0:DEEP, :] = rows(from_east, forcing_at, DEEP)
    turned[0:REACH, :] += weighted(rows(from_east, count_at, REACH), to_east)
    turned[LANES - DEEP : LANES, :] = rows(from_west, forcing_at, DEEP)
    turned[LANES - REACH : LANES, :] += weighted(rows(from_west, count_at + skip, REACH), to_west)
    turned[40 : 40 + EDGE, :] = sum(weights(rows(from_east, count_at, EDGE)))
    turned[40 - EDGE : 40, :] = sum(weights(rows(from_west, count_at, EDGE)))
    turned[60 : 60 + EDGE, :] = rows(from_east, pressure_at, EDGE)
    turned[60 - EDGE : 60, :] = rows(from_west, pressure_at, EDGE)
    turned[80 : 80 + REACH, :] = weighted(rows(to_west, count_at, REACH), from_west)
    turned[80 - REACH : 80, :] = weighted(rows(to_east, count_at + skip, REACH), from_east)

    for buf in (halo_depth, halo_guess):
        for at in (0, PAD + ext):
            buf[at : at + PAD, :] = jnp.zeros((PAD, LANES), jnp.float32)
    for at in (0, PAD + ext):
        for buf in (half, half_w, even_e, even_w, odd_e, odd_w):
            buf[:, at : at + PAD, :] = jnp.zeros((tiles + 1, PAD, LANES), jnp.float32)
    near = (lane < EDGE) | (lane >= LANES - EDGE)
    close = (lane < DEEP) | (lane >= LANES - DEEP)
    for at in range(0, turned.shape[1], LANES):
        upright[at : at + LANES, :] = jnp.transpose(turned[:, at : at + LANES])
    for e in range(0, ext, STEP):
        r = e + PAD
        tile = upright[e : e + STEP, :]
        halo_depth[r : r + STEP, :] = jnp.where(near, turn(tile, -40), 0.0)
        halo_guess[r : r + STEP, :] = jnp.where(near, turn(tile, -60), 0.0)
        halo_part[e : e + STEP, :] = jnp.where(close, tile, 0.0)
        fix[e : e + STEP, :] = turn(tile, -80)

    def span(i, by=0):
        return pl.ds(PAD + i * STEP + by, STEP)

    def strip(i):
        return pl.ds(pl.multiple_of(i * STEP, STEP), STEP)

    def read(main, halo, rows):
        return [main[t, rows, :] for t in range(tiles)] + [halo[rows, :]]

    shifted = ((even_e, even_w), (odd_e, odd_w))
    bases = (base0, base1, base2, base3, base4)
    both = range(tiles + 1)
    inner = height // STEP
    above = ROWS // STEP

    def put_beside(values, slot, i):
        east, west = neighbours(values, lane)
        for t in both:
            shifted[slot][0][t, span(i), :] = east[t]
            shifted[slot][1][t, span(i), :] = west[t]

    def prepare(i, c):
        low = [
            jnp.minimum(a, b)
            for a, b in zip(
                read(depth, halo_depth, span(i)), read(depth, halo_depth, span(i, 1))
            )
        ]
        east, west = neighbours(low, lane)
        corner = [0.5 * jnp.minimum(a, b) for a, b in zip(low, east)]
        west = [0.5 * jnp.minimum(a, b) for a, b in zip(low, west)]
        for t in both:
            half[t, span(i), :] = corner[t]
            half_w[t, span(i), :] = west[t]
        put_beside(read(guess, halo_guess, span(i)), 0, i)
        return c

    sweep(prepare, ext // STEP, WIDE)

    def around(slot, t, i):
        vec_e, vec_w = shifted[slot]
        return (
            (half[t, span(i), :], vec_e[t, span(i, 1), :]),
            (half_w[t, span(i), :], vec_w[t, span(i, 1), :]),
            (half[t, span(i, -1), :], vec_e[t, span(i, -1), :]),
            (half_w[t, span(i, -1), :], vec_w[t, span(i, -1), :]),
        )

    def begin(inside):
        def body(i, c):
            here = read(guess, halo_guess, span(i))
            wide = read(depth, halo_depth, span(i))
            fixes = fix[strip(i), :]
            values = []
            for t in both:
                (ch, ne), (chw, nw), (ch_s, se), (chw_s, sw) = around(0, t, i)
                diagonal = IMPLICIT + ((ch + chw) + (ch_s + chw_s))
                inv = 1.0 / diagonal
                inverse[t, strip(i), :] = inv
                image = IMPLICIT * here[t] + (
                    (ch * (here[t] - ne) + chw * (here[t] - nw))
                    + (ch_s * (here[t] - se) + chw_s * (here[t] - sw))
                )
                total = halo_part[strip(i), :] if t == tiles else part[t, strip(i), :]
                if t == 0:
                    total += jnp.where(lane < REACH, fixes, 0.0)
                if t == tiles - 1:
                    total += jnp.where(lane >= LANES - REACH, fixes, 0.0)
                side = jnp.where(wide[t] > 0.0, total + IMPLICIT * here[t], 0.0)
                values.append((side - image) * inv)
                if inside and t < tiles:
                    base0[t, strip(i - above), :] = values[t]
                    diag[t, strip(i - above), :] = diagonal
            put_beside(values, 1, i)
            return c

        return body

    sweep(begin(True), inner, WIDE_INNER, 0, above)
    sweep(begin(False), 2, 2, 0, 0, above + inner)

    zero = jnp.zeros((STEP, LANES), jnp.float32)

    sums = []
    for j in range(ITERS):
        final = j + 1 == ITERS

        def apply(inside, j=j, final=final):
            def body(i, carry):
                even, odd = carry
                values = []
                for t in both:
                    if final and t == tiles:
                        continue
                    (ch, ne), (chw, nw), (ch_s, se), (chw_s, sw) = around((j + 1) % 2, t, i)
                    value = inverse[t, strip(i), :] * (
                        (ch * ne + chw * nw) + (ch_s * se + chw_s * sw)
                    )
                    values.append(value)
                    if inside and t < tiles:
                        now = bases[j][t, strip(i - above), :]
                        scaled = diag[t, strip(i - above), :] * now
                        even = even + scaled * now
                        odd = odd + scaled * value
                        bases[j + 1][t, strip(i - above), :] = value
                if not final:
                    put_beside(values, j % 2, i)
                return even, odd

            return body

        sums += sweep(apply(True), inner, WIDE_INNER, (zero, zero), above)
        if not final:
            sweep(apply(False), 2, 2, (zero, zero), 0, above + inner)
    lane_row = lax.broadcasted_iota(jnp.int32, (1, LANES), 1)
    found = jnp.zeros((1, LANES), jnp.float32)
    for m in range(2 * ITERS):
        found = jnp.where(lane_row == m, jnp.sum(sums[m]), found)
    for d in range(moments.shape[0]):
        moments[d] = found


def combine_kernel(moments, guess, base0, base1, base2, base3, base4, diag, pressure, residual):
    height, width = pressure.shape
    total = jnp.sum(moments[...], axis=0)
    h = [jnp.broadcast_to(total[:, m : m + 1], (STEP, LANES)) for m in range(2 * ITERS)]
    one, zero = jnp.ones((STEP, LANES), jnp.float32), None

    def plus(a, b):
        return b if a is None else a if b is None else a + b

    def times(a, b):
        return None if a is None or b is None else a * b

    def minus_n(poly):
        moved = [zero] + list(poly)
        return [
            a if b is None else (-b if a is None else a - b)
            for a, b in zip(list(poly) + [zero], moved)
        ]

    def inner(left, right):
        total = None
        for i, a in enumerate(left):
            part = None
            for j, b in enumerate(right):
                part = plus(part, times(b, h[i + j]))
            total = plus(total, times(a, part))
        return total

    rest, direction, answer = [one], [one], []
    norm = h[0]
    for iteration in range(ITERS):
        image = minus_n(direction)
        alpha = norm / inner(direction, image)
        answer = [
            plus(answer[i] if i < len(answer) else None, alpha * c)
            for i, c in enumerate(direction)
        ]
        rest = [
            plus(rest[i] if i < len(rest) else None, -(alpha * c)) for i, c in enumerate(image)
        ]
        if iteration + 1 < ITERS:
            following = inner(rest, rest)
            ratio = following / norm
            direction = [
                plus(c, ratio * direction[i] if i < len(direction) else None)
                for i, c in enumerate(rest)
            ]
            norm = following
    bases = (base0, base1, base2, base3, base4)
    for t in range(width // LANES):
        for o in range(0, height, STEP):
            vecs = [b[t, o : o + STEP, :] for b in bases]
            moved = sum(c * v for c, v in zip(answer, vecs))
            left = sum(c * v for c, v in zip(rest, vecs))
            at = PAD + ROWS + o
            cols = pl.ds(t * LANES, LANES)
            pressure[o : o + STEP, cols] = guess[t, at : at + STEP, :] + moved
            residual[o : o + STEP, cols] = diag[t, o : o + STEP, :] * left


def shift(value, axis, by):
    size = lax.axis_size(axis)
    return lax.ppermute(value, axis, [(i, (i + by) % size) for i in range(size)])


def shards(fields, level_count, thickness, old_pressure):
    levels, height, width = fields.shape[1:]
    ext, tall = height + 2 * ROWS, height + LANES
    f32 = jnp.float32

    counts = level_count.astype(f32)

    def edge(at):
        pick = lambda a: lax.slice_in_dim(a, at, at + ROWS, axis=a.ndim - 2)
        flat = pick(fields).reshape(3 * levels, ROWS, width)
        return jnp.concatenate(
            [flat, pick(counts)[None], pick(old_pressure)[None]], axis=0
        )

    south = shift(edge(height - ROWS), "by", 1)
    north = shift(edge(0), "by", -1)

    message = message_rows(levels)[3]
    tiles, padded = width // LANES, ext + 2 * PAD
    smem = pl.BlockSpec(memory_space=pltpu.SMEM)
    vmem = pl.BlockSpec(memory_space=pltpu.VMEM)
    hbm = pl.BlockSpec(memory_space=pltpu.HBM)
    shaped = lambda *dims: jax.ShapeDtypeStruct(dims, f32)
    scratch = lambda *dims: pltpu.VMEM(dims, f32)
    main = (tiles, ext, LANES)
    loose = (tiles, padded, LANES)
    params = lambda size: pltpu.CompilerParams(vmem_limit_bytes=size)
    partial, outside = pl.pallas_call(
        inner_kernel,
        in_specs=[smem, hbm, vmem],
        out_specs=[vmem] * 2,
        out_shape=[shaped(*main), shaped(levels, height, LANES)],
        scratch_shapes=[
            scratch(levels, 3, tiles, height + 2 * PAD, LANES),
            scratch(levels, tiles + 1, height + 2 * PAD, LANES),
            scratch(levels, 3, tiles + 1, height, LANES),
            pltpu.SemaphoreType.DMA((levels, tiles)),
        ],
        compiler_params=params(INNER_GRANT),
        cost_estimate=pl.CostEstimate(
            flops=40 * fields.size // 3, bytes_accessed=4 * fields.size, transcendentals=0
        ),
        name="inner_forcing",
    )(thickness, fields, counts)

    results = (main, loose, loose, (message, tall), (message, tall))
    part, depth, guess, to_east, to_west = pl.pallas_call(
        edge_kernel,
        in_specs=[smem, hbm, vmem, vmem, vmem, hbm, vmem, vmem],
        out_specs=[vmem] * 5,
        out_shape=[shaped(*dims) for dims in results],
        scratch_shapes=[
            scratch(2, 3, levels, tiles, 3 * ROWS, LANES),
            scratch(2, levels, tiles + 1, 3 * ROWS, LANES),
            scratch(2, levels, 3, tiles + 1, STEP, LANES),
            scratch(levels, tall, LANES),
            scratch(*main),
            scratch(tall, LANES),
            scratch(height, width),
            pltpu.SemaphoreType.DMA((12 * tiles,)),
            pltpu.SemaphoreType.DMA((1,)),
        ],
        compiler_params=params(GRANT),
        name="edge_forcing",
    )(thickness, fields, south, north, counts, old_pressure, partial, outside)

    from_west = shift(to_east, "bx", 1)
    from_east = shift(to_west, "bx", -1)

    devices = lax.axis_size("by") * lax.axis_size("bx")
    *bases, diag, moments = pl.pallas_call(
        solve_kernel,
        in_specs=[smem] + [vmem] * 7,
        out_specs=[vmem] * (ITERS + 3),
        out_shape=[
            *[shaped(tiles, height, LANES)] * (ITERS + 2),
            shaped(devices, 1, LANES),
        ],
        scratch_shapes=[scratch(LANES, tall), scratch(tall, LANES)]
        + [scratch(ext, LANES)] * 2
        + [scratch(padded, LANES)] * 2
        + [scratch(tiles + 1, padded, LANES)] * 2
        + [scratch(tiles + 1, ext, LANES)]
        + [scratch(tiles + 1, padded, LANES)] * 4,
        compiler_params=pltpu.CompilerParams(vmem_limit_bytes=GRANT),
        name="krylov",
    )(thickness, part, depth, guess, to_east, to_west, from_west, from_east)

    moments = lax.all_to_all(moments, ("by", "bx"), split_axis=0, concat_axis=0, tiled=True)
    return tuple(
        pl.pallas_call(
            combine_kernel,
            in_specs=[vmem] * (ITERS + 4),
            out_specs=[vmem] * 2,
            out_shape=[shaped(height, width)] * 2,
            compiler_params=pltpu.CompilerParams(vmem_limit_bytes=GRANT),
            name="combine",
        )(moments, guess, *bases, diag)
    )


def solution(mesh):
    placed = (P(None, None, "by", "bx"), P("by", "bx"), P(), P("by", "bx"))
    return jax.shard_map(
        shards,
        mesh=mesh,
        in_specs=placed,
        out_specs=(P("by", "bx"), P("by", "bx")),
        check_vma=False,
    )
```

```python
import math

import jax
import jax.numpy as jnp
from jax import lax
from jax.experimental import pallas as pl
from jax.experimental.pallas import tpu as pltpu
from jax.sharding import PartitionSpec as P

ITERS = 4
VISCOSITY = 0.05
IMPLICIT = 0.05

ROWS = 8
PAD = 8
LANES = 128
REACH = 3
DEEP = ITERS
EDGE = ITERS + 1

STEP = 8
GRANT = 16 * 2**20
INNER_GRANT = 52 * 2**20
CHUNK = 32
WIDE = 34
WIDE_INNER = 32


def message_rows(levels):
    forcing_at = REACH * levels
    count_at = forcing_at + DEEP
    pressure_at = count_at + EDGE
    total = pressure_at + EDGE
    return forcing_at, count_at, pressure_at, -(-total // 8) * 8


def lane_index():
    return lax.broadcasted_iota(jnp.int32, (STEP, LANES), 1)


def turn(value, by):
    return pltpu.roll(value, by % LANES, 1)


def neighbours(tiles, lane, by=1, want_east=True, want_west=True):
    count = len(tiles)
    zero = jnp.zeros((STEP, LANES), jnp.float32)
    east = west = None
    if want_east:
        back = [zero if t is None else turn(t, -by) for t in tiles]
        east = [jnp.where(lane >= LANES - by, back[(i + 1) % count], back[i]) for i in range(count)]
    if want_west:
        forth = [zero if t is None else turn(t, by) for t in tiles]
        west = [jnp.where(lane < by, forth[i - 1], forth[i]) for i in range(count)]
    return east, west


def mix_strip(zonal, merid, mixed, row, lane):
    tiles = zonal.shape[0]
    near = lambda by=0: pl.ds(row + by, STEP)
    east, west = neighbours([zonal[t, near(), :] for t in range(tiles)] + [None], lane)
    for t in range(tiles + 1):
        value = east[t] - west[t]
        if t < tiles:
            value += merid[t, near(1), :] - merid[t, near(-1), :]
        mixed[t, near(), :] = value


def spread_strip(baro, mixed, row, out, at, lane):
    tiles = baro.shape[0]
    both = range(tiles + 1)
    near = lambda by=0: pl.ds(row + by, STEP)
    far, once = [], []
    for t in both:
        own = mixed[t, near(), :]
        beside = mixed[t, near(1), :] + mixed[t, near(-1), :]
        beyond = mixed[t, near(2), :] + mixed[t, near(-2), :]
        once.append(2.0 * beside - 8.0 * own)
        still = beyond - 8.0 * beside + 20.0 * own
        if t < tiles:
            pressure = 10.0 * baro[t, near(), :]
            around = baro[t, near(2), :] + baro[t, near(-2), :]
            own = own + pressure
            still += 10.0 * around - 4.0 * pressure
        far.append(own)
        out[2, t, at, :] = still
    east, west = neighbours(far, lane)
    for t in both:
        out[0, t, at, :] = once[t] + east[t]
        out[1, t, at, :] = once[t] + west[t]


def gather_strip(staged, at, lane):
    both = range(staged.shape[1])
    east, _ = neighbours([staged[0, t, at, :] for t in both], lane, 1, True, False)
    _, west = neighbours([staged[1, t, at, :] for t in both], lane, 1, False, True)
    return [staged[2, t, at, :] + (east[t] + west[t]) for t in both]


def sweep(body, strips, unroll, carry=0, first=0, stride=1):
    step = lambda i, c: body(first + stride * i, c)
    return lax.fori_loop(0, strips, step, carry, unroll=unroll)


def lane_tiles(tiles):
    return [pl.ds(t * LANES, LANES) for t in range(tiles)]


def inner_kernel(
    thick, fields, counts, part, beyond, block, mixed, staged, arrivals
):
    levels = fields.shape[1]
    height, width = counts.shape
    tiles = width // LANES
    lane = lane_index()
    cols = lane_tiles(tiles)
    strips = height // STEP
    size = math.gcd(strips, CHUNK)

    def arrival(at, t):
        return pltpu.make_async_copy(
            fields.at[:, at, :, cols[t]], block.at[at, :, t, pl.ds(PAD, height), :], arrivals.at[at, t]
        )

    for at in range(levels):
        for t in range(tiles):
            arrival(at, t).start()
    part[...] = jnp.zeros_like(part)

    def mix(n, c):
        chunks = strips // size
        level, chunk = lax.div(n, chunks), lax.rem(n, chunks)

        @pl.when(chunk == 0)
        def _():
            for t in range(tiles):
                arrival(level, t).wait()

        for q in range(size):
            row = PAD + pl.multiple_of(chunk * (size * STEP), STEP) + q * STEP
            mix_strip(block.at[level, 0], block.at[level, 1], mixed.at[level], row, lane)
        return c

    def chunked(body):
        chunks = strips // size

        def step(n, c):
            level, chunk = lax.div(n, chunks), lax.rem(n, chunks)
            for q in range(size):
                body(level, pl.multiple_of(chunk * (size * STEP), STEP) + q * STEP)
            return c

        sweep(step, levels * chunks, 2)

    def spread(level, row):
        at = pl.ds(row, STEP)
        spread_strip(block.at[level, 2], mixed.at[level], PAD + row, staged.at[level], at, lane)

    def weigh(level, row):
        at, rows = pl.ds(row, STEP), pl.ds(ROWS + row, STEP)
        total = gather_strip(staged.at[level], at, lane)
        number = level.astype(jnp.float32)
        for t in range(tiles):
            weight = jnp.where(counts[at, cols[t]] > number, thick[level], 0.0)
            part[t, rows, :] += weight * total[t]
        beyond[level, at, :] = total[tiles]

    sweep(mix, levels * (strips // size), 1)
    chunked(spread)
    chunked(weigh)


def edge_kernel(
    thick, fields, south, north, counts, old_hbm, part_in, beyond_in,
    part, depth, guess, to_east, to_west,
    block, mixed, staged, beyond, wet, edges, old, arrivals, others,
):
    levels = fields.shape[1]
    height, width = counts.shape
    tiles = width // LANES
    ext = height + 2 * ROWS
    forcing_at = message_rows(levels)[0]
    lane = lane_index()
    cols = lane_tiles(tiles)

    copies = [
        pltpu.make_async_copy(old_hbm, old, others.at[0]),
    ]
    for f in range(3):
        for t, c in enumerate(cols):
            for side, (here, there, halo, row) in enumerate(
                ((ROWS, 0, south, 0), (0, 2 * ROWS, north, height - 2 * ROWS))
            ):
                at = 4 * (f * tiles + t) + 2 * side
                group = block.at[side, f, :, t]
                copies += [
                    pltpu.make_async_copy(
                        fields.at[f, :, pl.ds(row, 2 * ROWS), c],
                        group.at[:, pl.ds(here, 2 * ROWS), :],
                        arrivals.at[at],
                    ),
                    pltpu.make_async_copy(
                        halo.at[pl.ds(f * levels, levels), :, c],
                        group.at[:, pl.ds(there, ROWS), :],
                        arrivals.at[at + 1],
                    ),
                ]
    for copy in copies:
        copy.start()
    low, high = slice(0, ROWS - DEEP), slice(ext - (ROWS - DEEP), ext)
    for buf in (depth, guess):
        for at in (0, PAD + ext):
            buf[:, at : at + PAD, :] = jnp.zeros((tiles, PAD, LANES), jnp.float32)
    inner = slice(2 * ROWS - DEEP, ext - (2 * ROWS - DEEP))
    part[:, inner, :] = part_in[:, inner, :]
    beyond[:, inner, :] = beyond_in[:, inner.start - ROWS : inner.stop - ROWS, :]
    for outer in (low, high):
        part[:, outer, :] = jnp.zeros((tiles, ROWS - DEEP, LANES), jnp.float32)
    for outer in (low, slice(high.start, beyond.shape[1])):
        beyond[:, outer, :] = jnp.zeros((levels, outer.stop - outer.start, LANES), jnp.float32)
    edges[ext:, :] = jnp.zeros((edges.shape[0] - ext, LANES), jnp.float32)
    for copy in copies:
        copy.wait()
    for t, c in enumerate(cols):
        wet[t, :ROWS, :] = south[3 * levels, :, c]
        wet[t, ROWS : ROWS + height, :] = counts[:, c]
        wet[t, ROWS + height :, :] = north[3 * levels, :, c]

    plans = ((ROWS - DEEP, (2, 10)), (2 * ROWS - DEEP, (10, 14)))
    starts = (ROWS - DEEP, ext - (2 * ROWS - DEEP))

    def mix(k, c):
        for side, (_, rows) in enumerate(plans):
            for row in rows:
                mix_strip(block.at[side, 0, k], block.at[side, 1, k], mixed.at[side, k], row, lane)
        return c

    every = pl.ds(0, STEP)

    def spread(k, c):
        for side, (row, _) in enumerate(plans):
            spread_strip(block.at[side, 2, k], mixed.at[side, k], row, staged.at[side, k], every, lane)
        return c

    def weigh(k, carry):
        found = []
        number, thickness = k.astype(jnp.float32), thick[k]
        for side, e in enumerate(starts):
            total = gather_strip(staged.at[side, k], every, lane)
            for t in range(tiles):
                weight = jnp.where(wet[t, e : e + STEP, :] > number, thickness, 0.0)
                found.append(weight * total[t])
            beyond[k, e : e + STEP, :] = total[tiles]
        return tuple(a + b for a, b in zip(carry, found))

    sweep(mix, levels, levels)
    sweep(spread, levels, levels)
    zero = jnp.zeros((STEP, LANES), jnp.float32)
    found = sweep(weigh, levels, levels, (zero,) * (2 * tiles))
    for side, e in enumerate(starts):
        for t in range(tiles):
            part[t, e : e + STEP, :] = found[side * tiles + t]

    scale = -0.5 * VISCOSITY
    for e in range(0, ext, STEP):
        r = e + PAD
        begin = []
        for t, c in enumerate(cols):
            if e < ROWS:
                pressure = south[3 * levels + 1, :, c]
            elif e >= ROWS + height:
                pressure = north[3 * levels + 1, :, c]
            else:
                pressure = old[e - ROWS : e - ROWS + STEP, c]
            counts = wet[t, e : e + STEP, :]
            depth[t, r : r + STEP, :] = sum(
                jnp.where(counts > float(k), thick[k], 0.0) for k in range(levels)
            )
            begin.append(jnp.where(counts > 0.0, pressure, 0.0))
            guess[t, r : r + STEP, :] = begin[t]
            part[t, e : e + STEP, :] *= scale
        tile = None
        for t, inside, start in ((tiles - 1, True, 0), (0, False, LANES // 2)):
            at = start
            for piece, size in (
                (part[t, e : e + STEP, :], DEEP),
                (wet[t, e : e + STEP, :], EDGE),
                (begin[t], EDGE),
            ):
                moved = turn(piece, at + size if inside else at)
                mask = (lane >= at) & (lane < at + size)
                tile = jnp.where(mask, moved, 0.0 if tile is None else tile)
                at += size
        edges[e : e + STEP, :] = tile
    size = DEEP + 2 * EDGE
    for message in (to_east, to_west):
        message[...] = jnp.zeros_like(message)
    for at in range(0, to_east.shape[1], LANES):
        span = slice(at, at + LANES)
        for k in range(levels):
            mine = slice(REACH * k, REACH * k + REACH)
            turned = scale * jnp.transpose(beyond[k, span, :])
            to_west[mine, span] = turned[LANES - REACH :, :]
            to_east[mine, span] = turned[:REACH, :]
        turned = jnp.transpose(edges[span, :])
        to_east[forcing_at : forcing_at + size, span] = turned[:size, :]
        to_west[forcing_at : forcing_at + size, span] = turned[LANES // 2 : LANES // 2 + size, :]


def solve_kernel(
    thick, part, depth, guess, to_east, to_west, from_west, from_east,
    base0, base1, base2, base3, base4, diag, moments,
    turned, upright, fix, halo_part, halo_depth, halo_guess, half, half_w, inverse, even_e, even_w, odd_e, odd_w,
):
    tiles, ext, _ = part.shape
    height = ext - 2 * ROWS
    levels = thick.shape[0]
    forcing_at, count_at, pressure_at, _ = message_rows(levels)
    lane = lane_index()

    def weights(counts):
        return [jnp.where(counts > float(k), thick[k], 0.0) for k in range(levels)]

    def weighted(counts, message):
        total = None
        for k, weight in enumerate(weights(counts)):
            term = weight * message[REACH * k : REACH * k + REACH, :]
            total = term if total is None else total + term
        return total

    def rows(message, at, size):
        return message[at : at + size, :]

    skip = EDGE - REACH
    turned[...] = jnp.zeros_like(turned)
    turned[0:DEEP, :] = rows(from_east, forcing_at, DEEP)
    turned[0:REACH, :] += weighted(rows(from_east, count_at, REACH), to_east)
    turned[LANES - DEEP : LANES, :] = rows(from_west, forcing_at, DEEP)
    turned[LANES - REACH : LANES, :] += weighted(rows(from_west, count_at + skip, REACH), to_west)
    turned[40 : 40 + EDGE, :] = sum(weights(rows(from_east, count_at, EDGE)))
    turned[40 - EDGE : 40, :] = sum(weights(rows(from_west, count_at, EDGE)))
    turned[60 : 60 + EDGE, :] = rows(from_east, pressure_at, EDGE)
    turned[60 - EDGE : 60, :] = rows(from_west, pressure_at, EDGE)
    turned[80 : 80 + REACH, :] = weighted(rows(to_west, count_at, REACH), from_west)
    turned[80 - REACH : 80, :] = weighted(rows(to_east, count_at + skip, REACH), from_east)

    for buf in (halo_depth, halo_guess):
        for at in (0, PAD + ext):
            buf[at : at + PAD, :] = jnp.zeros((PAD, LANES), jnp.float32)
    for at in (0, PAD + ext):
        for buf in (half, half_w, even_e, even_w, odd_e, odd_w):
            buf[:, at : at + PAD, :] = jnp.zeros((tiles + 1, PAD, LANES), jnp.float32)
    near = (lane < EDGE) | (lane >= LANES - EDGE)
    close = (lane < DEEP) | (lane >= LANES - DEEP)
    for at in range(0, turned.shape[1], LANES):
        upright[at : at + LANES, :] = jnp.transpose(turned[:, at : at + LANES])
    for e in range(0, ext, STEP):
        r = e + PAD
        tile = upright[e : e + STEP, :]
        halo_depth[r : r + STEP, :] = jnp.where(near, turn(tile, -40), 0.0)
        halo_guess[r : r + STEP, :] = jnp.where(near, turn(tile, -60), 0.0)
        halo_part[e : e + STEP, :] = jnp.where(close, tile, 0.0)
        fix[e : e + STEP, :] = turn(tile, -80)

    def span(i, by=0):
        return pl.ds(PAD + i * STEP + by, STEP)

    def strip(i):
        return pl.ds(pl.multiple_of(i * STEP, STEP), STEP)

    def read(main, halo, rows):
        return [main[t, rows, :] for t in range(tiles)] + [halo[rows, :]]

    shifted = ((even_e, even_w), (odd_e, odd_w))
    bases = (base0, base1, base2, base3, base4)
    both = range(tiles + 1)
    inner = height // STEP
    above = ROWS // STEP

    def put_beside(values, slot, i):
        east, west = neighbours(values, lane)
        for t in both:
            shifted[slot][0][t, span(i), :] = east[t]
            shifted[slot][1][t, span(i), :] = west[t]

    def prepare(i, c):
        low = [
            jnp.minimum(a, b)
            for a, b in zip(
                read(depth, halo_depth, span(i)), read(depth, halo_depth, span(i, 1))
            )
        ]
        east, west = neighbours(low, lane)
        corner = [0.5 * jnp.minimum(a, b) for a, b in zip(low, east)]
        west = [0.5 * jnp.minimum(a, b) for a, b in zip(low, west)]
        for t in both:
            half[t, span(i), :] = corner[t]
            half_w[t, span(i), :] = west[t]
        put_beside(read(guess, halo_guess, span(i)), 0, i)
        return c

    sweep(prepare, ext // STEP, WIDE)

    def around(slot, t, i):
        vec_e, vec_w = shifted[slot]
        return (
            (half[t, span(i), :], vec_e[t, span(i, 1), :]),
            (half_w[t, span(i), :], vec_w[t, span(i, 1), :]),
            (half[t, span(i, -1), :], vec_e[t, span(i, -1), :]),
            (half_w[t, span(i, -1), :], vec_w[t, span(i, -1), :]),
        )

    def begin(inside):
        def body(i, c):
            here = read(guess, halo_guess, span(i))
            wide = read(depth, halo_depth, span(i))
            fixes = fix[strip(i), :]
            values = []
            for t in both:
                (ch, ne), (chw, nw), (ch_s, se), (chw_s, sw) = around(0, t, i)
                diagonal = IMPLICIT + ((ch + chw) + (ch_s + chw_s))
                inv = 1.0 / diagonal
                inverse[t, strip(i), :] = inv
                image = IMPLICIT * here[t] + (
                    (ch * (here[t] - ne) + chw * (here[t] - nw))
                    + (ch_s * (here[t] - se) + chw_s * (here[t] - sw))
                )
                total = halo_part[strip(i), :] if t == tiles else part[t, strip(i), :]
                if t == 0:
                    total += jnp.where(lane < REACH, fixes, 0.0)
                if t == tiles - 1:
                    total += jnp.where(lane >= LANES - REACH, fixes, 0.0)
                side = jnp.where(wide[t] > 0.0, total + IMPLICIT * here[t], 0.0)
                values.append((side - image) * inv)
                if inside and t < tiles:
                    base0[t, strip(i - above), :] = values[t]
                    diag[t, strip(i - above), :] = diagonal
            put_beside(values, 1, i)
            return c

        return body

    sweep(begin(True), inner, WIDE_INNER, 0, above)
    sweep(begin(False), 2, 2, 0, 0, above + inner)

    zero = jnp.zeros((STEP, LANES), jnp.float32)

    sums = []
    for j in range(ITERS):
        final = j + 1 == ITERS

        def apply(inside, j=j, final=final):
            def body(i, carry):
                even, odd = carry
                values = []
                for t in both:
                    if final and t == tiles:
                        continue
                    (ch, ne), (chw, nw), (ch_s, se), (chw_s, sw) = around((j + 1) % 2, t, i)
                    value = inverse[t, strip(i), :] * (
                        (ch * ne + chw * nw) + (ch_s * se + chw_s * sw)
                    )
                    values.append(value)
                    if inside and t < tiles:
                        now = bases[j][t, strip(i - above), :]
                        scaled = diag[t, strip(i - above), :] * now
                        even = even + scaled * now
                        odd = odd + scaled * value
                        bases[j + 1][t, strip(i - above), :] = value
                if not final:
                    put_beside(values, j % 2, i)
                return even, odd

            return body

        sums += sweep(apply(True), inner, WIDE_INNER, (zero, zero), above)
        if not final:
            sweep(apply(False), 2, 2, (zero, zero), 0, above + inner)
    lane_row = lax.broadcasted_iota(jnp.int32, (1, LANES), 1)
    found = jnp.zeros((1, LANES), jnp.float32)
    for m in range(2 * ITERS):
        found = jnp.where(lane_row == m, jnp.sum(sums[m]), found)
    for d in range(moments.shape[0]):
        moments[d] = found


def combine_kernel(moments, guess, base0, base1, base2, base3, base4, diag, pressure, residual):
    height, width = pressure.shape
    total = jnp.sum(moments[...], axis=0)
    h = [jnp.broadcast_to(total[:, m : m + 1], (STEP, LANES)) for m in range(2 * ITERS)]
    one, zero = jnp.ones((STEP, LANES), jnp.float32), None

    def plus(a, b):
        return b if a is None else a if b is None else a + b

    def times(a, b):
        return None if a is None or b is None else a * b

    def minus_n(poly):
        moved = [zero] + list(poly)
        return [
            a if b is None else (-b if a is None else a - b)
            for a, b in zip(list(poly) + [zero], moved)
        ]

    def inner(left, right):
        total = None
        for i, a in enumerate(left):
            part = None
            for j, b in enumerate(right):
                part = plus(part, times(b, h[i + j]))
            total = plus(total, times(a, part))
        return total

    rest, direction, answer = [one], [one], []
    norm = h[0]
    for iteration in range(ITERS):
        image = minus_n(direction)
        alpha = norm / inner(direction, image)
        answer = [
            plus(answer[i] if i < len(answer) else None, alpha * c)
            for i, c in enumerate(direction)
        ]
        rest = [
            plus(rest[i] if i < len(rest) else None, -(alpha * c)) for i, c in enumerate(image)
        ]
        if iteration + 1 < ITERS:
            following = inner(rest, rest)
            ratio = following / norm
            direction = [
                plus(c, ratio * direction[i] if i < len(direction) else None)
                for i, c in enumerate(rest)
            ]
            norm = following
    bases = (base0, base1, base2, base3, base4)
    for t in range(width // LANES):
        cols = pl.ds(t * LANES, LANES)

        def join(i, c, t=t, cols=cols):
            rows = pl.ds(pl.multiple_of(i * STEP, STEP), STEP)
            vecs = [b[t, rows, :] for b in bases]
            moved = sum(c * v for c, v in zip(answer, vecs))
            left = sum(c * v for c, v in zip(rest, vecs))
            there = pl.ds(pl.multiple_of(PAD + ROWS + i * STEP, STEP), STEP)
            pressure[rows, cols] = guess[t, there, :] + moved
            residual[rows, cols] = diag[t, rows, :] * left
            return c

        sweep(join, height // STEP, 8)


def shift(value, axis, by):
    size = lax.axis_size(axis)
    return lax.ppermute(value, axis, [(i, (i + by) % size) for i in range(size)])


def shards(fields, level_count, thickness, old_pressure):
    levels, height, width = fields.shape[1:]
    ext, tall = height + 2 * ROWS, height + LANES
    f32 = jnp.float32

    counts = level_count.astype(f32)

    def edge(at):
        pick = lambda a: lax.slice_in_dim(a, at, at + ROWS, axis=a.ndim - 2)
        flat = pick(fields).reshape(3 * levels, ROWS, width)
        return jnp.concatenate(
            [flat, pick(counts)[None], pick(old_pressure)[None]], axis=0
        )

    south = shift(edge(height - ROWS), "by", 1)
    north = shift(edge(0), "by", -1)

    message = message_rows(levels)[3]
    tiles, padded = width // LANES, ext + 2 * PAD
    smem = pl.BlockSpec(memory_space=pltpu.SMEM)
    vmem = pl.BlockSpec(memory_space=pltpu.VMEM)
    hbm = pl.BlockSpec(memory_space=pltpu.HBM)
    shaped = lambda *dims: jax.ShapeDtypeStruct(dims, f32)
    scratch = lambda *dims: pltpu.VMEM(dims, f32)
    main = (tiles, ext, LANES)
    loose = (tiles, padded, LANES)
    params = lambda size: pltpu.CompilerParams(vmem_limit_bytes=size)
    partial, outside = pl.pallas_call(
        inner_kernel,
        in_specs=[smem, hbm, vmem],
        out_specs=[vmem] * 2,
        out_shape=[shaped(*main), shaped(levels, height, LANES)],
        scratch_shapes=[
            scratch(levels, 3, tiles, height + 2 * PAD, LANES),
            scratch(levels, tiles + 1, height + 2 * PAD, LANES),
            scratch(levels, 3, tiles + 1, height, LANES),
            pltpu.SemaphoreType.DMA((levels, tiles)),
        ],
        compiler_params=params(INNER_GRANT),
        cost_estimate=pl.CostEstimate(
            flops=40 * fields.size // 3, bytes_accessed=4 * fields.size, transcendentals=0
        ),
        name="inner_forcing",
    )(thickness, fields, counts)

    results = (main, loose, loose, (message, tall), (message, tall))
    part, depth, guess, to_east, to_west = pl.pallas_call(
        edge_kernel,
        in_specs=[smem, hbm, vmem, vmem, vmem, hbm, vmem, vmem],
        out_specs=[vmem] * 5,
        out_shape=[shaped(*dims) for dims in results],
        scratch_shapes=[
            scratch(2, 3, levels, tiles, 3 * ROWS, LANES),
            scratch(2, levels, tiles + 1, 3 * ROWS, LANES),
            scratch(2, levels, 3, tiles + 1, STEP, LANES),
            scratch(levels, tall, LANES),
            scratch(*main),
            scratch(tall, LANES),
            scratch(height, width),
            pltpu.SemaphoreType.DMA((12 * tiles,)),
            pltpu.SemaphoreType.DMA((1,)),
        ],
        compiler_params=params(GRANT),
        name="edge_forcing",
    )(thickness, fields, south, north, counts, old_pressure, partial, outside)

    from_west = shift(to_east, "bx", 1)
    from_east = shift(to_west, "bx", -1)

    devices = lax.axis_size("by") * lax.axis_size("bx")
    *bases, diag, moments = pl.pallas_call(
        solve_kernel,
        in_specs=[smem] + [vmem] * 7,
        out_specs=[vmem] * (ITERS + 3),
        out_shape=[
            *[shaped(tiles, height, LANES)] * (ITERS + 2),
            shaped(devices, 1, LANES),
        ],
        scratch_shapes=[scratch(LANES, tall), scratch(tall, LANES)]
        + [scratch(ext, LANES)] * 2
        + [scratch(padded, LANES)] * 2
        + [scratch(tiles + 1, padded, LANES)] * 2
        + [scratch(tiles + 1, ext, LANES)]
        + [scratch(tiles + 1, padded, LANES)] * 4,
        compiler_params=pltpu.CompilerParams(vmem_limit_bytes=GRANT),
        name="krylov",
    )(thickness, part, depth, guess, to_east, to_west, from_west, from_east)

    moments = lax.all_to_all(moments, ("by", "bx"), split_axis=0, concat_axis=0, tiled=True)
    return tuple(
        pl.pallas_call(
            combine_kernel,
            in_specs=[vmem] * (ITERS + 4),
            out_specs=[vmem] * 2,
            out_shape=[shaped(height, width)] * 2,
            compiler_params=pltpu.CompilerParams(vmem_limit_bytes=GRANT),
            name="combine",
        )(moments, guess, *bases, diag)
    )


def solution(mesh):
    placed = (P(None, None, "by", "bx"), P("by", "bx"), P(), P("by", "bx"))
    return jax.shard_map(
        shards,
        mesh=mesh,
        in_specs=placed,
        out_specs=(P("by", "bx"), P("by", "bx")),
        check_vma=False,
    )
```
